512 devices in a mesh: term: 16 (over y, z_hi, core), sector: 32 (over x, z_lo).
Axes of the slice: x: 4, y: 4, z: 16 (z_hi: 2, z_lo: 8; z = z_hi * 8 + z_lo), core: 2. Of those that a mesh axis runs over, the one named last changes fastest.
Arguments:
- psi_blocks: float32 [128, 128, 128], P('sector'), may hold values from -6 to 6
- left_ops: float32 [16, 128, 128, 128], P('term', 'sector'), may hold values from -0.5 to 0.5
- right_ops: float32 [16, 128, 128, 128], P('term', 'sector'), may hold values from -0.5 to 0.5
- couplings: float32 [16, 16], replicated, may hold values from -1.5 to 1.5
- pattern: int32 [16, 128], P(None, 'sector'), may hold values from 0 to 1, as said below
- channel: int32 [16], replicated, may hold values from 0 to 7
- target: int32 [128, 8], P('sector'), may hold values from 0 to 127, as said below
Outputs:
- sigma_blocks: float32 [128, 128, 128], P('sector', 'term')
The draws below stay inside these ranges and needn't reach their ends.
Inputs may be any that keep to these rules, and one draw needn't show every extreme that they name: `pattern`: only 0 and 1. `target`: of the 32 entries of the rows 4 j to 4 j + 3, at most 2 name sectors in one aligned group of 4 sectors, and exactly 2 do for some group, for every j.
All inputs are finite; a program needn't handle non-finite values.
Results may differ from the reference program's by a relative error of at most 0.0003.
Values sent between devices are 32-bit elements; how exact they have to be, the bound alone decides.
A program may use at most 64 MiB of HBM per device.

```python
import jax
import jax.numpy as jnp
from jax import lax

B = 128
K = 8
SEC_DEV = 4
CAP = 2
TERMS = 16
SECT = 128


def draw_pattern(key, part):
    key_level, key_roll = jax.random.split(jax.random.fold_in(key, 11))
    levels = jax.random.randint(key_level, (1, SECT), 1, 5)
    rolled = jax.random.randint(key_roll, (TERMS, SECT), 0, 4)
    return (rolled < levels).astype(jnp.int32)


def draw_target(key, part):
    slot_count = SEC_DEV * K
    groups = SECT // SEC_DEV

    def one_group(group_key):
        key_first, key_second, key_third = jax.random.split(group_key, 3)
        chosen = jax.random.permutation(key_first, groups)
        owners = jnp.repeat(chosen, CAP)[:slot_count]
        owners = jax.random.permutation(key_second, owners)
        inside = jax.random.randint(key_third, (slot_count,), 0, SEC_DEV)
        return owners * SEC_DEV + inside
    group_keys = jax.random.split(jax.random.fold_in(key, 23), groups)
    rows_all = jax.vmap(one_group)(group_keys)
    return rows_all.reshape(SECT, K).astype(jnp.int32)


def plant(result, own_key, smallest, high):
    longest = result.shape.index(max(result.shape))
    spots = []
    for shift in (0, 1):
        where = [jax.random.randint(jax.random.fold_in(own_key, axis), (), 0, length) for axis, length in enumerate(result.shape)]
        where[longest] = (where[longest] + shift) % result.shape[longest]
        spots.append(tuple(where))
    return result.at[spots[0]].set(smallest).at[spots[1]].set(high)


def block_scale(stream_key, dims, cuts, low, largest):
    level, own = 1.0, jax.random.fold_in(stream_key, 6)
    for position, shards_of in cuts:
        heights = jnp.exp(jax.random.uniform(jax.random.fold_in(own, position), (shards_of,), jnp.float32, low / len(cuts), largest / len(cuts)))
        level = level * jnp.repeat(heights, dims[position] // shards_of).reshape([-1 if axis == position else 1 for axis in range(len(dims))])
    return level


def scatter_about(key, extent, spread, bound, cuts=(), kind=jnp.bfloat16):
    array = spread * jax.random.normal(key, extent, jnp.float32)
    if cuts:
        array = array * block_scale(key, extent, cuts, -0.22, 0.18)
    return jnp.clip(array, -bound, bound).astype(kind)


def setup_inputs(seed: int = 0) -> dict:
    keys = jax.random.split(jax.random.key(seed), 8)
    psi_blocks = scatter_about(keys[0], (SECT, B, B), 1.0, 6.0, ((0, 32),), jnp.float32)
    left_ops = scatter_about(keys[1], (TERMS, SECT, B, B), B ** -0.5, 0.5, ((0, 16), (1, 32)), jnp.float32)
    right_ops = scatter_about(keys[2], (TERMS, SECT, B, B), B ** -0.5, 0.5, ((0, 16), (1, 32)), jnp.float32)
    couplings = scatter_about(keys[3], (TERMS, TERMS), TERMS ** -0.5, 1.5, (), jnp.float32)
    pattern = draw_pattern(jax.random.fold_in(keys[7], 71), 0)
    channel = plant(jax.random.randint(keys[5], (TERMS,), 0, K), jax.random.fold_in(keys[5], 1), 0, K - 1).astype(jnp.int32)
    target = draw_target(jax.random.fold_in(keys[7], 71), 0)
    return dict(psi_blocks=psi_blocks, left_ops=left_ops, right_ops=right_ops, couplings=couplings, pattern=pattern, channel=channel, target=target)


PRECISE = lax.Precision.HIGHEST


def reference(psi_blocks, left_ops, right_ops, couplings, pattern, channel, target):
    def per_sector(sigma_all, sector):
        block = psi_blocks[sector]
        rights = right_ops[:, sector]
        lefts = left_ops[:, sector]

        def per_term(totals, term_id):
            def live_path(current):
                comp = jnp.einsum("b,bij->ij", couplings[term_id], rights, precision=PRECISE)
                inner_prod = jnp.dot(block, comp, precision=PRECISE)
                term_value = jnp.dot(lefts[term_id], inner_prod, precision=PRECISE)
                return current.at[channel[term_id]].add(term_value)

            return lax.cond(pattern[term_id, sector] > 0, live_path, lambda current: current, totals), None

        partial_value, _ = lax.scan(per_term, jnp.zeros((K, B, B), jnp.float32), jnp.arange(TERMS, dtype=jnp.int32))
        return sigma_all.at[target[sector]].add(partial_value), None

    sigma_all, _ = lax.scan(per_sector, jnp.zeros((SECT, B, B), jnp.float32), jnp.arange(SECT, dtype=jnp.int32))
    return sigma_all
```

```python
import jax
import jax.numpy as jnp
from jax import lax
from jax.sharding import PartitionSpec as P

PRECISE = lax.Precision.HIGHEST


def route_to_owners(slices, target):
    sec_dev, channels, share_rows, block_size = slices.shape
    slot_count = sec_dev * channels
    row_length = share_rows * block_size
    flat_rows = slices.reshape(slot_count, row_length)
    targets = target.reshape(slot_count)
    owners = lax.axis_size("sector")
    capacity = max(2, (slot_count + owners - 1) // owners)
    destination = targets // sec_dev
    slot_order = jnp.arange(slot_count, dtype=jnp.int32)
    earlier = (destination[None, :] == destination[:, None]) & (
        slot_order[None, :] < slot_order[:, None]
    )
    slot_rank = jnp.sum(earlier.astype(jnp.int32), axis=1)
    position = destination * capacity + slot_rank
    buffer_rows = jnp.arange(owners * capacity, dtype=jnp.int32)
    placing = (buffer_rows[:, None] == position[None, :]).astype(jnp.float32)
    outgoing = jnp.dot(placing, flat_rows, precision=PRECISE, preferred_element_type=jnp.float32)
    labels = jnp.dot(
        placing,
        (targets % sec_dev + 1).astype(jnp.float32),
        precision=PRECISE,
        preferred_element_type=jnp.float32,
    )
    incoming = lax.all_to_all(outgoing, "sector", split_axis=0, concat_axis=0, tiled=True)
    in_labels = lax.all_to_all(labels, "sector", split_axis=0, concat_axis=0, tiled=True)
    local_ids = (jnp.arange(sec_dev, dtype=jnp.int32) + 1).astype(jnp.float32)
    picking = (in_labels[None, :] == local_ids[:, None]).astype(jnp.float32)
    result = jnp.dot(picking, incoming, precision=PRECISE, preferred_element_type=jnp.float32)
    return result.reshape(sec_dev, share_rows, block_size)


def local(psi_blocks, left_ops, right_ops, couplings, pattern, channel, target):
    sec_dev, block_size, _ = psi_blocks.shape
    terms = couplings.shape[0]
    channels = target.shape[1]
    share_rows = block_size // terms

    rights = right_ops[0].reshape(sec_dev, terms, share_rows, block_size)
    rights = lax.all_to_all(rights, "term", split_axis=1, concat_axis=1, tiled=True)
    comp_rows = jnp.einsum("ab,sbrk->sark", couplings, rights, precision=PRECISE)
    comp_rows = lax.all_to_all(comp_rows, "term", split_axis=1, concat_axis=1, tiled=True)
    comp = comp_rows.reshape(sec_dev, block_size, block_size)

    inner = jnp.einsum("sij,sjk->sik", psi_blocks, comp, precision=PRECISE)
    contrib = jnp.einsum("sij,sjk->sik", left_ops[0], inner, precision=PRECISE)

    contrib = contrib.reshape(sec_dev, terms, share_rows, block_size)
    contrib = lax.all_to_all(contrib, "term", split_axis=1, concat_axis=1, tiled=True)
    chan_ids = jnp.arange(channels, dtype=jnp.int32)
    select = (channel[None, :] == chan_ids[:, None]).astype(jnp.float32)
    weights = select[None, :, :] * pattern.T.astype(jnp.float32)[:, None, :]
    partial = jnp.einsum("sca,sark->scrk", weights, contrib, precision=PRECISE)
    return route_to_owners(partial, target)


def solution(mesh):
    placed = (
        P("sector", None, None),
        P("term", "sector", None, None),
        P("term", "sector", None, None),
        P(),
        P(None, "sector"),
        P(),
        P("sector", None),
    )
    return jax.shard_map(
        local, mesh=mesh, in_specs=placed, out_specs=P("sector", "term", None), check_vma=False
    )
```

```python
import functools

import jax
import jax.numpy as jnp
from jax import lax
from jax.experimental import pallas as pl
from jax.experimental.pallas import tpu as pltpu
from jax.sharding import PartitionSpec as P

MESH = pl.DeviceIdType.MESH

PRECISE = lax.Precision.HIGHEST


def exchange_kernel(axis, n, split, x_ref, o_ref, send_sem, recv_sem, local_sem):
    me = lax.axis_index(axis)
    barrier = pltpu.get_barrier_semaphore()
    for k in range(1, n):
        pl.semaphore_signal(barrier, inc=1, device_id={axis: lax.rem(me + k, n)}, device_id_type=MESH)
    pl.semaphore_wait(barrier, n - 1)

    def part(ref, idx):
        return ref.at[idx] if split == 0 else ref.at[:, idx]

    local = pltpu.make_async_copy(part(x_ref, me), part(o_ref, me), local_sem)
    local.start()
    copies = []
    for k in range(1, n):
        peer = lax.rem(me + k, n)
        copy = pltpu.make_async_remote_copy(
            src_ref=part(x_ref, peer),
            dst_ref=part(o_ref, me),
            send_sem=send_sem.at[k],
            recv_sem=recv_sem.at[k],
            device_id={axis: peer},
            device_id_type=MESH,
        )
        copy.start()
        copies.append(copy)
    local.wait()
    for copy in copies:
        copy.wait()


def exchange(x, axis, split, collective_id):
    n = x.shape[split]
    return pl.pallas_call(
        functools.partial(exchange_kernel, axis, n, split),
        out_shape=jax.ShapeDtypeStruct(x.shape, x.dtype),
        in_specs=[pl.BlockSpec(memory_space=pltpu.VMEM)],
        out_specs=pl.BlockSpec(memory_space=pltpu.VMEM),
        scratch_shapes=[
            pltpu.SemaphoreType.DMA((n,)),
            pltpu.SemaphoreType.DMA((n,)),
            pltpu.SemaphoreType.DMA(()),
        ],
        compiler_params=pltpu.CompilerParams(collective_id=collective_id, has_side_effects=True),
    )(x)


def route_to_owners(slices, target):
    sec_dev, channels, share_rows, block_size = slices.shape
    slot_count = sec_dev * channels
    row_length = share_rows * block_size
    flat_rows = slices.reshape(slot_count, row_length)
    targets = target.reshape(slot_count)
    owners = lax.axis_size("sector")
    capacity = max(2, (slot_count + owners - 1) // owners)
    destination = targets // sec_dev
    slot_order = jnp.arange(slot_count, dtype=jnp.int32)
    earlier = (destination[None, :] == destination[:, None]) & (
        slot_order[None, :] < slot_order[:, None]
    )
    slot_rank = jnp.sum(earlier.astype(jnp.int32), axis=1)
    position = destination * capacity + slot_rank
    buffer_rows = jnp.arange(owners * capacity, dtype=jnp.int32)
    placing = (buffer_rows[:, None] == position[None, :]).astype(jnp.float32)
    outgoing = jnp.dot(placing, flat_rows, precision=PRECISE, preferred_element_type=jnp.float32)
    labels = jnp.dot(
        placing,
        (targets % sec_dev + 1).astype(jnp.float32),
        precision=PRECISE,
        preferred_element_type=jnp.float32,
    )
    slot_rows = outgoing.reshape(owners, capacity * share_rows, block_size)
    label_row = jnp.zeros((owners, 8, block_size), jnp.float32)
    label_row = label_row.at[:, 0, :capacity].set(labels.reshape(owners, capacity))
    packed = jnp.concatenate([slot_rows, label_row], axis=1)
    packed = exchange(packed, "sector", 0, 3)
    incoming = packed[:, : capacity * share_rows].reshape(owners * capacity, row_length)
    in_labels = packed[:, capacity * share_rows, :capacity].reshape(owners * capacity)
    local_ids = (jnp.arange(sec_dev, dtype=jnp.int32) + 1).astype(jnp.float32)
    picking = (in_labels[None, :] == local_ids[:, None]).astype(jnp.float32)
    result = jnp.dot(picking, incoming, precision=PRECISE, preferred_element_type=jnp.float32)
    return result.reshape(sec_dev, share_rows, block_size)


def local(psi_blocks, left_ops, right_ops, couplings, pattern, channel, target):
    sec_dev, block_size, _ = psi_blocks.shape
    terms = couplings.shape[0]
    channels = target.shape[1]
    share_rows = block_size // terms

    rights = right_ops[0].reshape(sec_dev, terms, share_rows, block_size)
    rights = exchange(rights, "term", 1, 0)
    comp_rows = jnp.einsum("ab,sbrk->sark", couplings, rights, precision=PRECISE)
    comp_rows = exchange(comp_rows, "term", 1, 1)
    comp = comp_rows.reshape(sec_dev, block_size, block_size)

    inner = jnp.einsum("sij,sjk->sik", psi_blocks, comp, precision=PRECISE)
    contrib = jnp.einsum("sij,sjk->sik", left_ops[0], inner, precision=PRECISE)

    contrib = contrib.reshape(sec_dev, terms, share_rows, block_size)
    contrib = exchange(contrib, "term", 1, 2)
    chan_ids = jnp.arange(channels, dtype=jnp.int32)
    select = (channel[None, :] == chan_ids[:, None]).astype(jnp.float32)
    weights = select[None, :, :] * pattern.T.astype(jnp.float32)[:, None, :]
    partial = jnp.einsum("sca,sark->scrk", weights, contrib, precision=PRECISE)
    return route_to_owners(partial, target)


def solution(mesh):
    placed = (
        P("sector", None, None),
        P("term", "sector", None, None),
        P("term", "sector", None, None),
        P(),
        P(None, "sector"),
        P(),
        P("sector", None),
    )
    return jax.shard_map(
        local, mesh=mesh, in_specs=placed, out_specs=P("sector", "term", None), check_vma=False
    )
```

```python
import functools

import jax
import jax.numpy as jnp
from jax import lax
from jax.experimental import pallas as pl
from jax.experimental.pallas import tpu as pltpu
from jax.sharding import PartitionSpec as P

MESH = pl.DeviceIdType.MESH

PRECISE = lax.Precision.HIGHEST


def exchange_kernel(axis, n, split, x_ref, o_ref, send_sem, recv_sem, local_sem):
    me = lax.axis_index(axis)
    barrier = pltpu.get_barrier_semaphore()
    for k in range(1, n):
        pl.semaphore_signal(barrier, inc=1, device_id={axis: lax.rem(me + k, n)}, device_id_type=MESH)
    pl.semaphore_wait(barrier, n - 1)

    def part(ref, idx):
        return ref.at[idx] if split == 0 else ref.at[:, idx]

    local = pltpu.make_async_copy(part(x_ref, me), part(o_ref, me), local_sem)
    local.start()
    copies = []
    for k in range(1, n):
        peer = lax.rem(me + k, n)
        copy = pltpu.make_async_remote_copy(
            src_ref=part(x_ref, peer),
            dst_ref=part(o_ref, me),
            send_sem=send_sem.at[k],
            recv_sem=recv_sem.at[k],
            device_id={axis: peer},
            device_id_type=MESH,
        )
        copy.start()
        copies.append(copy)
    local.wait()
    for copy in copies:
        copy.wait()


def exchange(x, axis, split, collective_id):
    n = x.shape[split]
    return pl.pallas_call(
        functools.partial(exchange_kernel, axis, n, split),
        out_shape=jax.ShapeDtypeStruct(x.shape, x.dtype),
        in_specs=[pl.BlockSpec(memory_space=pltpu.VMEM)],
        out_specs=pl.BlockSpec(memory_space=pltpu.VMEM),
        scratch_shapes=[
            pltpu.SemaphoreType.DMA((n,)),
            pltpu.SemaphoreType.DMA((n,)),
            pltpu.SemaphoreType.DMA(()),
        ],
        compiler_params=pltpu.CompilerParams(collective_id=collective_id, has_side_effects=True),
    )(x)


def route_to_owners(slices, target):
    sec_dev, channels, share_rows, block_size = slices.shape
    slot_count = sec_dev * channels
    row_length = share_rows * block_size
    flat_rows = slices.reshape(slot_count, row_length)
    targets = target.reshape(slot_count)
    owners = lax.axis_size("sector")
    capacity = max(2, (slot_count + owners - 1) // owners)
    destination = targets // sec_dev
    slot_order = jnp.arange(slot_count, dtype=jnp.int32)
    earlier = (destination[None, :] == destination[:, None]) & (
        slot_order[None, :] < slot_order[:, None]
    )
    slot_rank = jnp.sum(earlier.astype(jnp.int32), axis=1)
    position = destination * capacity + slot_rank
    buffer_rows = jnp.arange(owners * capacity, dtype=jnp.int32)
    placing = (buffer_rows[:, None] == position[None, :]).astype(jnp.float32)
    outgoing = jnp.dot(placing, flat_rows, precision=PRECISE, preferred_element_type=jnp.float32)
    labels = jnp.dot(
        placing,
        (targets % sec_dev + 1).astype(jnp.float32),
        precision=PRECISE,
        preferred_element_type=jnp.float32,
    )
    slot_rows = outgoing.reshape(owners, capacity * share_rows, block_size)
    label_row = jnp.zeros((owners, 1, block_size), jnp.float32)
    label_row = label_row.at[:, 0, :capacity].set(labels.reshape(owners, capacity))
    packed = jnp.concatenate([slot_rows, label_row], axis=1)
    packed = exchange(packed, "sector", 0, 3)
    incoming = packed[:, : capacity * share_rows].reshape(owners * capacity, row_length)
    in_labels = packed[:, capacity * share_rows, :capacity].reshape(owners * capacity)
    local_ids = (jnp.arange(sec_dev, dtype=jnp.int32) + 1).astype(jnp.float32)
    picking = (in_labels[None, :] == local_ids[:, None]).astype(jnp.float32)
    result = jnp.dot(picking, incoming, precision=PRECISE, preferred_element_type=jnp.float32)
    return result.reshape(sec_dev, share_rows, block_size)


def local(psi_blocks, left_ops, right_ops, couplings, pattern, channel, target):
    sec_dev, block_size, _ = psi_blocks.shape
    terms = couplings.shape[0]
    channels = target.shape[1]
    share_rows = block_size // terms

    rights = right_ops[0].reshape(sec_dev, terms, share_rows, block_size)
    rights = exchange(rights, "term", 1, 0)
    comp_rows = jnp.einsum("ab,sbrk->sark", couplings, rights, precision=PRECISE)
    comp_rows = exchange(comp_rows, "term", 1, 1)
    comp = comp_rows.reshape(sec_dev, block_size, block_size)

    inner = jnp.einsum("sij,sjk->sik", psi_blocks, comp, precision=PRECISE)
    contrib = jnp.einsum("sij,sjk->sik", left_ops[0], inner, precision=PRECISE)

    contrib = contrib.reshape(sec_dev, terms, share_rows, block_size)
    contrib = exchange(contrib, "term", 1, 2)
    chan_ids = jnp.arange(channels, dtype=jnp.int32)
    select = (channel[None, :] == chan_ids[:, None]).astype(jnp.float32)
    weights = select[None, :, :] * pattern.T.astype(jnp.float32)[:, None, :]
    partial = jnp.einsum("sca,sark->scrk", weights, contrib, precision=PRECISE)
    return route_to_owners(partial, target)


def solution(mesh):
    placed = (
        P("sector", None, None),
        P("term", "sector", None, None),
        P("term", "sector", None, None),
        P(),
        P(None, "sector"),
        P(),
        P("sector", None),
    )
    return jax.shard_map(
        local, mesh=mesh, in_specs=placed, out_specs=P("sector", "term", None), check_vma=False
    )
```

```python
import functools
import math

import jax
import jax.numpy as jnp
from jax import lax
from jax.experimental import pallas as pl
from jax.experimental.pallas import tpu as pltpu
from jax.sharding import PartitionSpec as P

MESH = pl.DeviceIdType.MESH

PRECISE = lax.Precision.HIGHEST


def exchange_kernel(axis, n, split, x_ref, o_ref, send_sem, recv_sem, local_sem):
    me = lax.axis_index(axis)
    barrier = pltpu.get_barrier_semaphore()
    for k in range(1, n):
        pl.semaphore_signal(barrier, inc=1, device_id={axis: lax.rem(me + k, n)}, device_id_type=MESH)
    pl.semaphore_wait(barrier, n - 1)

    def part(ref, idx):
        return ref.at[idx] if split == 0 else ref.at[:, idx]

    local = pltpu.make_async_copy(part(x_ref, me), part(o_ref, me), local_sem)
    local.start()
    copies = []
    for k in range(1, n):
        peer = lax.rem(me + k, n)
        copy = pltpu.make_async_remote_copy(
            src_ref=part(x_ref, peer),
            dst_ref=part(o_ref, me),
            send_sem=send_sem.at[k],
            recv_sem=recv_sem.at[k],
            device_id={axis: peer},
            device_id_type=MESH,
        )
        copy.start()
        copies.append(copy)
    local.wait()
    for copy in copies:
        copy.wait()


def exchange(x, axis, split, collective_id):
    n = x.shape[split]
    return pl.pallas_call(
        functools.partial(exchange_kernel, axis, n, split),
        out_shape=jax.ShapeDtypeStruct(x.shape, x.dtype),
        in_specs=[pl.BlockSpec(memory_space=pltpu.VMEM)],
        out_specs=pl.BlockSpec(memory_space=pltpu.VMEM),
        scratch_shapes=[
            pltpu.SemaphoreType.DMA((n,)),
            pltpu.SemaphoreType.DMA((n,)),
            pltpu.SemaphoreType.DMA(()),
        ],
        compiler_params=pltpu.CompilerParams(collective_id=collective_id, has_side_effects=True),
    )(x)


def rows_of(index, share_rows):
    return pl.ds(pl.multiple_of(index * share_rows, share_rows), share_rows)


def term_kernel(
    n, r_ref, l_ref, psi_ref, coup_ref, wts_ref, out_ref,
    got_right, comp_rows, comp, contrib, got_contrib, send_sem, recv_sem, local_sem,
):
    me = lax.axis_index("term")
    sec_dev, _, share_rows, block_size = got_right.shape
    channels = out_ref.shape[1]
    barrier = pltpu.get_barrier_semaphore()
    for k in range(1, n):
        pl.semaphore_signal(barrier, inc=1, device_id={"term": lax.rem(me + k, n)}, device_id_type=MESH)
    pl.semaphore_wait(barrier, n - 1)

    def send(stage, s, src_of, dst):
        local = pltpu.make_async_copy(src_of(me), dst, local_sem.at[stage, s])
        local.start()
        copies = [local]
        for k in range(1, n):
            peer = lax.rem(me + k, n)
            copy = pltpu.make_async_remote_copy(
                src_ref=src_of(peer),
                dst_ref=dst,
                send_sem=send_sem.at[stage, s, k],
                recv_sem=recv_sem.at[stage, s, k],
                device_id={"term": peer},
                device_id_type=MESH,
            )
            copy.start()
            copies.append(copy)
        return copies

    def arrived(copies):
        copies[0].wait()
        for copy in copies[1:]:
            copy.wait_recv()

    def gathered(buf, s, k):
        return buf[s, lax.rem(me + k, n)]

    first = [send(0, s, lambda p, s=s: r_ref.at[s, rows_of(p, share_rows)], got_right.at[s, me]) for s in range(sec_dev)]
    second = []
    for s in range(sec_dev):
        arrived(first[s])
        parts = [gathered(got_right, s, k) for k in range(n)]
        for a in range(n):
            total = coup_ref[a * n] * parts[0]
            for k in range(1, n):
                total = total + coup_ref[a * n + k] * parts[k]
            comp_rows[s, a] = total
        second.append(send(1, s, lambda p, s=s: comp_rows.at[s, p], comp.at[s, rows_of(me, share_rows)]))
    third = []
    for s in range(sec_dev):
        arrived(second[s])
        inner = jnp.dot(psi_ref[s], comp[s], precision=PRECISE, preferred_element_type=jnp.float32)
        contrib[s] = jnp.dot(l_ref[s], inner, precision=PRECISE, preferred_element_type=jnp.float32)
        third.append(send(2, s, lambda p, s=s: contrib.at[s, rows_of(p, share_rows)], got_contrib.at[s, me]))
    for s in range(sec_dev):
        arrived(third[s])
        parts = [gathered(got_contrib, s, k) for k in range(n)]
        for c in range(channels):
            base = (s * channels + c) * n
            total = wts_ref[base] * parts[0]
            for k in range(1, n):
                total = total + wts_ref[base + k] * parts[k]
            out_ref[s, c] = total
    for copies in first + second + third:
        for copy in copies[1:]:
            copy.wait_send()


def term_stage(rights, lefts, psi_blocks, coup, wts, channels):
    sec_dev, block_size, _ = psi_blocks.shape
    n = math.isqrt(coup.shape[0])
    share_rows = block_size // n
    tiles = (sec_dev, n, share_rows, block_size)
    vmem = pl.BlockSpec(memory_space=pltpu.VMEM)
    smem = pl.BlockSpec(memory_space=pltpu.SMEM)
    return pl.pallas_call(
        functools.partial(term_kernel, n),
        out_shape=jax.ShapeDtypeStruct((sec_dev, channels, share_rows, block_size), jnp.float32),
        in_specs=[vmem, vmem, vmem, smem, smem],
        out_specs=vmem,
        scratch_shapes=[
            pltpu.VMEM(tiles, jnp.float32),
            pltpu.VMEM(tiles, jnp.float32),
            pltpu.VMEM((sec_dev, block_size, block_size), jnp.float32),
            pltpu.VMEM((sec_dev, block_size, block_size), jnp.float32),
            pltpu.VMEM(tiles, jnp.float32),
            pltpu.SemaphoreType.DMA((3, sec_dev, n)),
            pltpu.SemaphoreType.DMA((3, sec_dev, n)),
            pltpu.SemaphoreType.DMA((3, sec_dev)),
        ],
        compiler_params=pltpu.CompilerParams(collective_id=0, has_side_effects=True),
    )(rights, lefts, psi_blocks, coup, wts)


def route_to_owners(slices, target):
    sec_dev, channels, share_rows, block_size = slices.shape
    slot_count = sec_dev * channels
    row_length = share_rows * block_size
    flat_rows = slices.reshape(slot_count, row_length)
    targets = target.reshape(slot_count)
    owners = lax.axis_size("sector")
    capacity = max(2, (slot_count + owners - 1) // owners)
    destination = targets // sec_dev
    slot_order = jnp.arange(slot_count, dtype=jnp.int32)
    earlier = (destination[None, :] == destination[:, None]) & (
        slot_order[None, :] < slot_order[:, None]
    )
    slot_rank = jnp.sum(earlier.astype(jnp.int32), axis=1)
    position = destination * capacity + slot_rank
    buffer_rows = jnp.arange(owners * capacity, dtype=jnp.int32)
    placing = (buffer_rows[:, None] == position[None, :]).astype(jnp.float32)
    outgoing = jnp.dot(placing, flat_rows, precision=PRECISE, preferred_element_type=jnp.float32)
    labels = jnp.dot(
        placing,
        (targets % sec_dev + 1).astype(jnp.float32),
        precision=PRECISE,
        preferred_element_type=jnp.float32,
    )
    slot_rows = outgoing.reshape(owners, capacity * share_rows, block_size)
    label_row = jnp.zeros((owners, 1, block_size), jnp.float32)
    label_row = label_row.at[:, 0, :capacity].set(labels.reshape(owners, capacity))
    packed = jnp.concatenate([slot_rows, label_row], axis=1)
    packed = exchange(packed, "sector", 0, 1)
    incoming = packed[:, : capacity * share_rows].reshape(owners * capacity, row_length)
    in_labels = packed[:, capacity * share_rows, :capacity].reshape(owners * capacity)
    local_ids = (jnp.arange(sec_dev, dtype=jnp.int32) + 1).astype(jnp.float32)
    picking = (in_labels[None, :] == local_ids[:, None]).astype(jnp.float32)
    result = jnp.dot(picking, incoming, precision=PRECISE, preferred_element_type=jnp.float32)
    return result.reshape(sec_dev, share_rows, block_size)


def local(psi_blocks, left_ops, right_ops, couplings, pattern, channel, target):
    terms = couplings.shape[0]
    channels = target.shape[1]
    me = lax.axis_index("term")
    order = lax.rem(me + jnp.arange(terms, dtype=jnp.int32), terms)
    coup = couplings[:, order].reshape(-1)
    chan_ids = jnp.arange(channels, dtype=jnp.int32)
    select = (channel[None, :] == chan_ids[:, None]).astype(jnp.float32)
    weights = select[None, :, :] * pattern.T.astype(jnp.float32)[:, None, :]
    wts = weights[:, :, order].reshape(-1)
    partial = term_stage(right_ops[0], left_ops[0], psi_blocks, coup, wts, channels)
    return route_to_owners(partial, target)


def solution(mesh):
    placed = (
        P("sector", None, None),
        P("term", "sector", None, None),
        P("term", "sector", None, None),
        P(),
        P(None, "sector"),
        P(),
        P("sector", None),
    )
    return jax.shard_map(
        local, mesh=mesh, in_specs=placed, out_specs=P("sector", "term", None), check_vma=False
    )
```

```python
import functools

import jax
import jax.numpy as jnp
from jax import lax
from jax.experimental import pallas as pl
from jax.experimental.pallas import tpu as pltpu
from jax.sharding import PartitionSpec as P

MESH = pl.DeviceIdType.MESH

PRECISE = lax.Precision.HIGHEST


def exchange_kernel(axis, n, split, x_ref, o_ref, send_sem, recv_sem, local_sem):
    me = lax.axis_index(axis)
    barrier = pltpu.get_barrier_semaphore()
    for k in range(1, n):
        pl.semaphore_signal(barrier, inc=1, device_id={axis: lax.rem(me + k, n)}, device_id_type=MESH)
    pl.semaphore_wait(barrier, n - 1)

    def part(ref, idx):
        return ref.at[idx] if split == 0 else ref.at[:, idx]

    local = pltpu.make_async_copy(part(x_ref, me), part(o_ref, me), local_sem)
    local.start()
    copies = []
    for k in range(1, n):
        peer = lax.rem(me + k, n)
        copy = pltpu.make_async_remote_copy(
            src_ref=part(x_ref, peer),
            dst_ref=part(o_ref, me),
            send_sem=send_sem.at[k],
            recv_sem=recv_sem.at[k],
            device_id={axis: peer},
            device_id_type=MESH,
        )
        copy.start()
        copies.append(copy)
    local.wait()
    for copy in copies:
        copy.wait()


def exchange(x, axis, split, collective_id):
    n = x.shape[split]
    return pl.pallas_call(
        functools.partial(exchange_kernel, axis, n, split),
        out_shape=jax.ShapeDtypeStruct(x.shape, x.dtype),
        in_specs=[pl.BlockSpec(memory_space=pltpu.VMEM)],
        out_specs=pl.BlockSpec(memory_space=pltpu.VMEM),
        scratch_shapes=[
            pltpu.SemaphoreType.DMA((n,)),
            pltpu.SemaphoreType.DMA((n,)),
            pltpu.SemaphoreType.DMA(()),
        ],
        compiler_params=pltpu.CompilerParams(collective_id=collective_id, has_side_effects=True),
    )(x)


def rows_of(index, share_rows):
    return pl.ds(pl.multiple_of(index * share_rows, share_rows), share_rows)


def term_kernel(
    n, r_ref, l_hbm, psi_hbm, coup_ref, pattern_ref, channel_ref, out_ref,
    l_ref, psi_ref, got_right, comp_rows, comp, contrib, got_contrib, send_sem, recv_sem, local_sem, load_sem,
):
    me = lax.axis_index("term")
    sec_dev, _, share_rows, block_size = got_right.shape
    channels = out_ref.shape[1]
    barrier = pltpu.get_barrier_semaphore()
    for k in range(1, n):
        pl.semaphore_signal(barrier, inc=1, device_id={"term": lax.rem(me + k, n)}, device_id_type=MESH)
    pl.semaphore_wait(barrier, n - 1)

    def send(stage, s, src_of, dst):
        local = pltpu.make_async_copy(src_of(me), dst, local_sem.at[stage, s])
        local.start()
        copies = [local]
        for k in range(1, n):
            peer = lax.rem(me + k, n)
            copy = pltpu.make_async_remote_copy(
                src_ref=src_of(peer),
                dst_ref=dst,
                send_sem=send_sem.at[stage, s, k],
                recv_sem=recv_sem.at[stage, s, k],
                device_id={"term": peer},
                device_id_type=MESH,
            )
            copy.start()
            copies.append(copy)
        return copies

    def arrived(copies):
        copies[0].wait()
        for copy in copies[1:]:
            copy.wait_recv()

    def gathered(buf, s, k):
        return buf[s, lax.rem(me + k, n)]

    loads = [pltpu.make_async_copy(l_hbm, l_ref, load_sem.at[0]), pltpu.make_async_copy(psi_hbm, psi_ref, load_sem.at[1])]
    for load in loads:
        load.start()
    first = [send(0, s, lambda p, s=s: r_ref.at[s, rows_of(p, share_rows)], got_right.at[s, me]) for s in range(sec_dev)]
    second = []
    for s in range(sec_dev):
        arrived(first[s])
        parts = [gathered(got_right, s, k) for k in range(n)]
        for a in range(n):
            total = coup_ref[a, me] * parts[0]
            for k in range(1, n):
                total = total + coup_ref[a, lax.rem(me + k, n)] * parts[k]
            comp_rows[s, a] = total
        second.append(send(1, s, lambda p, s=s: comp_rows.at[s, p], comp.at[s, rows_of(me, share_rows)]))
    for load in loads:
        load.wait()
    third = []
    for s in range(sec_dev):
        arrived(second[s])
        inner = jnp.dot(psi_ref[s], comp[s], precision=PRECISE, preferred_element_type=jnp.float32)
        contrib[s] = jnp.dot(l_ref[s], inner, precision=PRECISE, preferred_element_type=jnp.float32)
        third.append(send(2, s, lambda p, s=s: contrib.at[s, rows_of(p, share_rows)], got_contrib.at[s, me]))
    for s in range(sec_dev):
        arrived(third[s])
        parts = [gathered(got_contrib, s, k) for k in range(n)]
        for c in range(channels):
            total = None
            for k in range(n):
                term = lax.rem(me + k, n)
                live = jnp.where(channel_ref[term] == c, pattern_ref[term, s], 0).astype(jnp.float32)
                total = live * parts[k] if total is None else total + live * parts[k]
            out_ref[s, c] = total
    for copies in first + second + third:
        for copy in copies[1:]:
            copy.wait_send()


def term_stage(rights, lefts, psi_blocks, couplings, pattern, channel, channels):
    sec_dev, block_size, _ = psi_blocks.shape
    n = couplings.shape[0]
    share_rows = block_size // n
    tiles = (sec_dev, n, share_rows, block_size)
    blocks = (sec_dev, block_size, block_size)
    hbm = pl.BlockSpec(memory_space=pl.ANY)
    smem = pl.BlockSpec(memory_space=pltpu.SMEM)
    return pl.pallas_call(
        functools.partial(term_kernel, n),
        out_shape=jax.ShapeDtypeStruct((sec_dev, channels, share_rows, block_size), jnp.float32),
        in_specs=[hbm, hbm, hbm, smem, smem, smem],
        out_specs=pl.BlockSpec(memory_space=pltpu.VMEM),
        scratch_shapes=[
            pltpu.VMEM(blocks, jnp.float32),
            pltpu.VMEM(blocks, jnp.float32),
            pltpu.VMEM(tiles, jnp.float32),
            pltpu.VMEM(tiles, jnp.float32),
            pltpu.VMEM(blocks, jnp.float32),
            pltpu.VMEM(blocks, jnp.float32),
            pltpu.VMEM(tiles, jnp.float32),
            pltpu.SemaphoreType.DMA((3, sec_dev, n)),
            pltpu.SemaphoreType.DMA((3, sec_dev, n)),
            pltpu.SemaphoreType.DMA((3, sec_dev)),
            pltpu.SemaphoreType.DMA((2,)),
        ],
        compiler_params=pltpu.CompilerParams(collective_id=0, has_side_effects=True),
    )(rights, lefts, psi_blocks, couplings, pattern, channel)


def route_to_owners(slices, target):
    sec_dev, channels, share_rows, block_size = slices.shape
    slot_count = sec_dev * channels
    row_length = share_rows * block_size
    flat_rows = slices.reshape(slot_count, row_length)
    targets = target.reshape(slot_count)
    owners = lax.axis_size("sector")
    capacity = max(2, (slot_count + owners - 1) // owners)
    destination = targets // sec_dev
    slot_order = jnp.arange(slot_count, dtype=jnp.int32)
    earlier = (destination[None, :] == destination[:, None]) & (
        slot_order[None, :] < slot_order[:, None]
    )
    slot_rank = jnp.sum(earlier.astype(jnp.int32), axis=1)
    position = destination * capacity + slot_rank
    buffer_rows = jnp.arange(owners * capacity, dtype=jnp.int32)
    placing = (buffer_rows[:, None] == position[None, :]).astype(jnp.float32)
    outgoing = jnp.dot(placing, flat_rows, precision=PRECISE, preferred_element_type=jnp.float32)
    labels = jnp.dot(
        placing,
        (targets % sec_dev + 1).astype(jnp.float32),
        precision=PRECISE,
        preferred_element_type=jnp.float32,
    )
    slot_rows = outgoing.reshape(owners, capacity * share_rows, block_size)
    label_row = jnp.zeros((owners, 1, block_size), jnp.float32)
    label_row = label_row.at[:, 0, :capacity].set(labels.reshape(owners, capacity))
    packed = jnp.concatenate([slot_rows, label_row], axis=1)
    packed = exchange(packed, "sector", 0, 1)
    incoming = packed[:, : capacity * share_rows].reshape(owners * capacity, row_length)
    in_labels = packed[:, capacity * share_rows, :capacity].reshape(owners * capacity)
    local_ids = (jnp.arange(sec_dev, dtype=jnp.int32) + 1).astype(jnp.float32)
    picking = (in_labels[None, :] == local_ids[:, None]).astype(jnp.float32)
    result = jnp.dot(picking, incoming, precision=PRECISE, preferred_element_type=jnp.float32)
    return result.reshape(sec_dev, share_rows, block_size)


def local(psi_blocks, left_ops, right_ops, couplings, pattern, channel, target):
    channels = target.shape[1]
    partial = term_stage(right_ops[0], left_ops[0], psi_blocks, couplings, pattern, channel, channels)
    return route_to_owners(partial, target)


def solution(mesh):
    placed = (
        P("sector", None, None),
        P("term", "sector", None, None),
        P("term", "sector", None, None),
        P(),
        P(None, "sector"),
        P(),
        P("sector", None),
    )
    return jax.shard_map(
        local, mesh=mesh, in_specs=placed, out_specs=P("sector", "term", None), check_vma=False
    )
```

```python
import functools

import jax
import jax.numpy as jnp
from jax import lax
from jax.experimental import pallas as pl
from jax.experimental.pallas import tpu as pltpu
from jax.sharding import PartitionSpec as P

MESH = pl.DeviceIdType.MESH

PRECISE = lax.Precision.HIGHEST


def rows_of(index, share_rows):
    return pl.ds(pl.multiple_of(index * share_rows, share_rows), share_rows)


def term_kernel(
    n, owners, r_ref, l_hbm, psi_hbm, coup_ref, pattern_ref, channel_ref, source_ref, keep_ref, label_ref,
    got_slots, got_labels,
    l_ref, psi_ref, got_right, comp_rows, comp, contrib, got_contrib, partial, outgoing,
    send_sem, recv_sem, local_sem, load_sem, route_sem, label_sem,
):
    me = lax.axis_index("term")
    here = lax.axis_index("sector")
    sec_dev, _, share_rows, block_size = got_right.shape
    channels = partial.shape[0] // sec_dev
    capacity = outgoing.shape[1] // share_rows
    barrier = pltpu.get_barrier_semaphore()
    for k in range(1, n):
        pl.semaphore_signal(barrier, inc=1, device_id={"term": lax.rem(me + k, n)}, device_id_type=MESH)
    for k in range(1, owners):
        pl.semaphore_signal(barrier, inc=1, device_id={"sector": lax.rem(here + k, owners)}, device_id_type=MESH)
    pl.semaphore_wait(barrier, n - 1 + owners - 1)

    def route(src_of, dst, sems, local):
        first = pltpu.make_async_copy(src_of(here), dst, local)
        first.start()
        copies = [first]
        for k in range(1, owners):
            peer = lax.rem(here + k, owners)
            copy = pltpu.make_async_remote_copy(
                src_ref=src_of(peer),
                dst_ref=dst,
                send_sem=sems.at[0, k],
                recv_sem=sems.at[1, k],
                device_id={"sector": peer},
                device_id_type=MESH,
            )
            copy.start()
            copies.append(copy)
        return copies

    labels = route(lambda p: label_ref.at[p], got_labels.at[here], label_sem, load_sem.at[2])

    def send(stage, s, src_of, dst):
        local = pltpu.make_async_copy(src_of(me), dst, local_sem.at[stage, s])
        local.start()
        copies = [local]
        for k in range(1, n):
            peer = lax.rem(me + k, n)
            copy = pltpu.make_async_remote_copy(
                src_ref=src_of(peer),
                dst_ref=dst,
                send_sem=send_sem.at[stage, s, k],
                recv_sem=recv_sem.at[stage, s, k],
                device_id={"term": peer},
                device_id_type=MESH,
            )
            copy.start()
            copies.append(copy)
        return copies

    def arrived(copies):
        copies[0].wait()
        for copy in copies[1:]:
            copy.wait_recv()

    def gathered(buf, s, k):
        return buf[s, lax.rem(me + k, n)]

    loads = [pltpu.make_async_copy(l_hbm, l_ref, load_sem.at[0]), pltpu.make_async_copy(psi_hbm, psi_ref, load_sem.at[1])]
    for load in loads:
        load.start()
    first = [send(0, s, lambda p, s=s: r_ref.at[s, rows_of(p, share_rows)], got_right.at[s, me]) for s in range(sec_dev)]
    second = []
    for s in range(sec_dev):
        arrived(first[s])
        parts = [gathered(got_right, s, k) for k in range(n)]
        for a in range(n):
            total = coup_ref[a, me] * parts[0]
            for k in range(1, n):
                total = total + coup_ref[a, lax.rem(me + k, n)] * parts[k]
            comp_rows[s, a] = total
        second.append(send(1, s, lambda p, s=s: comp_rows.at[s, p], comp.at[s, rows_of(me, share_rows)]))
    for load in loads:
        load.wait()
    third = []
    for s in range(sec_dev):
        arrived(second[s])
        inner = jnp.dot(psi_ref[s], comp[s], precision=PRECISE, preferred_element_type=jnp.float32)
        contrib[s] = jnp.dot(l_ref[s], inner, precision=PRECISE, preferred_element_type=jnp.float32)
        third.append(send(2, s, lambda p, s=s: contrib.at[s, rows_of(p, share_rows)], got_contrib.at[s, me]))
    for s in range(sec_dev):
        arrived(third[s])
        parts = [gathered(got_contrib, s, k) for k in range(n)]
        for c in range(channels):
            total = None
            for k in range(n):
                term = lax.rem(me + k, n)
                live = jnp.where(channel_ref[term] == c, pattern_ref[term, s], 0).astype(jnp.float32)
                total = live * parts[k] if total is None else total + live * parts[k]
            partial[s * channels + c] = total
    for o in range(owners):
        for slot in range(capacity):
            at = o * capacity + slot
            outgoing[o, pl.ds(slot * share_rows, share_rows)] = keep_ref[at] * partial[source_ref[at]]
    fourth = route(lambda p: outgoing.at[p], got_slots.at[here], route_sem, load_sem.at[3])
    for copies in (labels, fourth):
        arrived(copies)
    for copies in first + second + third + [labels, fourth]:
        for copy in copies[1:]:
            copy.wait_send()


def term_stage(rights, lefts, psi_blocks, couplings, pattern, channel, source, keep, label_rows, channels):
    sec_dev, block_size, _ = psi_blocks.shape
    n = couplings.shape[0]
    owners = label_rows.shape[0]
    capacity = source.shape[0] // owners
    share_rows = block_size // n
    tiles = (sec_dev, n, share_rows, block_size)
    blocks = (sec_dev, block_size, block_size)
    routed = (owners, capacity * share_rows, block_size)
    hbm = pl.BlockSpec(memory_space=pl.ANY)
    smem = pl.BlockSpec(memory_space=pltpu.SMEM)
    vmem = pl.BlockSpec(memory_space=pltpu.VMEM)
    return pl.pallas_call(
        functools.partial(term_kernel, n, owners),
        out_shape=(
            jax.ShapeDtypeStruct(routed, jnp.float32),
            jax.ShapeDtypeStruct(label_rows.shape, jnp.float32),
        ),
        in_specs=[hbm, hbm, hbm, smem, smem, smem, smem, smem, vmem],
        out_specs=(vmem, vmem),
        scratch_shapes=[
            pltpu.VMEM(blocks, jnp.float32),
            pltpu.VMEM(blocks, jnp.float32),
            pltpu.VMEM(tiles, jnp.float32),
            pltpu.VMEM(tiles, jnp.float32),
            pltpu.VMEM(blocks, jnp.float32),
            pltpu.VMEM(blocks, jnp.float32),
            pltpu.VMEM(tiles, jnp.float32),
            pltpu.VMEM((sec_dev * channels, share_rows, block_size), jnp.float32),
            pltpu.VMEM(routed, jnp.float32),
            pltpu.SemaphoreType.DMA((3, sec_dev, n)),
            pltpu.SemaphoreType.DMA((3, sec_dev, n)),
            pltpu.SemaphoreType.DMA((3, sec_dev)),
            pltpu.SemaphoreType.DMA((4,)),
            pltpu.SemaphoreType.DMA((2, owners)),
            pltpu.SemaphoreType.DMA((2, owners)),
        ],
        compiler_params=pltpu.CompilerParams(collective_id=0, has_side_effects=True),
    )(rights, lefts, psi_blocks, couplings, pattern, channel, source, keep, label_rows)


def slot_tables(target, owners):
    sec_dev, channels = target.shape
    slot_count = sec_dev * channels
    targets = target.reshape(slot_count)
    capacity = max(2, (slot_count + owners - 1) // owners)
    destination = targets // sec_dev
    slot_order = jnp.arange(slot_count, dtype=jnp.int32)
    earlier = (destination[None, :] == destination[:, None]) & (slot_order[None, :] < slot_order[:, None])
    position = destination * capacity + jnp.sum(earlier.astype(jnp.int32), axis=1)
    buffer_rows = jnp.arange(owners * capacity, dtype=jnp.int32)
    placing = buffer_rows[:, None] == position[None, :]
    keep = jnp.any(placing, axis=1)
    source = jnp.sum(jnp.where(placing, slot_order[None, :], 0), axis=1)
    labels = jnp.sum(jnp.where(placing, (targets % sec_dev + 1)[None, :], 0), axis=1)
    label_rows = jnp.zeros((owners, 1, 128), jnp.float32)
    label_rows = label_rows.at[:, 0, :capacity].set(labels.reshape(owners, capacity).astype(jnp.float32))
    return source.astype(jnp.int32), keep.astype(jnp.float32), label_rows


def pick_arrivals(got_slots, got_labels, sec_dev, capacity):
    owners, rows, block_size = got_slots.shape
    share_rows = rows // capacity
    incoming = got_slots.reshape(owners * capacity, share_rows * block_size)
    in_labels = got_labels[:, 0, :capacity].reshape(owners * capacity)
    local_ids = (jnp.arange(sec_dev, dtype=jnp.int32) + 1).astype(jnp.float32)
    picking = (in_labels[None, :] == local_ids[:, None]).astype(jnp.float32)
    result = jnp.dot(picking, incoming, precision=PRECISE, preferred_element_type=jnp.float32)
    return result.reshape(sec_dev, share_rows, block_size)


def local(psi_blocks, left_ops, right_ops, couplings, pattern, channel, target):
    sec_dev, channels = target.shape
    owners = lax.axis_size("sector")
    source, keep, label_rows = slot_tables(target, owners)
    got_slots, got_labels = term_stage(
        right_ops[0], left_ops[0], psi_blocks, couplings, pattern, channel, source, keep, label_rows, channels
    )
    return pick_arrivals(got_slots, got_labels, sec_dev, source.shape[0] // owners)


def solution(mesh):
    placed = (
        P("sector", None, None),
        P("term", "sector", None, None),
        P("term", "sector", None, None),
        P(),
        P(None, "sector"),
        P(),
        P("sector", None),
    )
    return jax.shard_map(
        local, mesh=mesh, in_specs=placed, out_specs=P("sector", "term", None), check_vma=False
    )
```

```python
import functools

import jax
import jax.numpy as jnp
from jax import lax
from jax.experimental import pallas as pl
from jax.experimental.pallas import tpu as pltpu
from jax.sharding import PartitionSpec as P

MESH = pl.DeviceIdType.MESH

PRECISE = lax.Precision.HIGHEST


def rows_of(index, share_rows):
    return pl.ds(pl.multiple_of(index * share_rows, share_rows), share_rows)


def term_kernel(
    n, owners, r_ref, l_hbm, psi_hbm, coup_ref, pattern_ref, channel_ref, source_ref, label_ref,
    got_slots, got_labels,
    l_ref, psi_ref, got_right, comp_rows, comp, contrib, got_contrib, partial, outgoing,
    send_sem, recv_sem, local_sem, load_sem, route_sem, label_sem,
):
    me = lax.axis_index("term")
    here = lax.axis_index("sector")
    sec_dev, _, share_rows, block_size = got_right.shape
    channels = (partial.shape[0] - 1) // sec_dev
    capacity = outgoing.shape[1] // share_rows
    barrier = pltpu.get_barrier_semaphore()
    for k in range(1, n):
        pl.semaphore_signal(barrier, inc=1, device_id={"term": lax.rem(me + k, n)}, device_id_type=MESH)
    for k in range(1, owners):
        pl.semaphore_signal(barrier, inc=1, device_id={"sector": lax.rem(here + k, owners)}, device_id_type=MESH)
    pl.semaphore_wait(barrier, n - 1 + owners - 1)

    def route(src_of, dst, sems, local):
        first = pltpu.make_async_copy(src_of(here), dst, local)
        first.start()
        copies = [first]
        for k in range(1, owners):
            peer = lax.rem(here + k, owners)
            copy = pltpu.make_async_remote_copy(
                src_ref=src_of(peer),
                dst_ref=dst,
                send_sem=sems.at[0, k],
                recv_sem=sems.at[1, k],
                device_id={"sector": peer},
                device_id_type=MESH,
            )
            copy.start()
            copies.append(copy)
        return copies

    labels = route(lambda p: label_ref.at[p], got_labels.at[here], label_sem, load_sem.at[2])

    def send(stage, s, src_of, dst):
        local = pltpu.make_async_copy(src_of(me), dst, local_sem.at[stage, s])
        local.start()
        copies = [local]
        for k in range(1, n):
            peer = lax.rem(me + k, n)
            copy = pltpu.make_async_remote_copy(
                src_ref=src_of(peer),
                dst_ref=dst,
                send_sem=send_sem.at[stage, s, k],
                recv_sem=recv_sem.at[stage, s, k],
                device_id={"term": peer},
                device_id_type=MESH,
            )
            copy.start()
            copies.append(copy)
        return copies

    def arrived(copies):
        copies[0].wait()
        for copy in copies[1:]:
            copy.wait_recv()

    def gathered(buf, s, k):
        return buf[s, lax.rem(me + k, n)]

    loads = [pltpu.make_async_copy(l_hbm, l_ref, load_sem.at[0]), pltpu.make_async_copy(psi_hbm, psi_ref, load_sem.at[1])]
    for load in loads:
        load.start()
    first = [send(0, s, lambda p, s=s: r_ref.at[s, rows_of(p, share_rows)], got_right.at[s, me]) for s in range(sec_dev)]
    second = []
    for s in range(sec_dev):
        arrived(first[s])
        parts = [gathered(got_right, s, k) for k in range(n)]
        for a in range(n):
            total = coup_ref[a, me] * parts[0]
            for k in range(1, n):
                total = total + coup_ref[a, lax.rem(me + k, n)] * parts[k]
            comp_rows[s, a] = total
        second.append(send(1, s, lambda p, s=s: comp_rows.at[s, p], comp.at[s, rows_of(me, share_rows)]))
    for load in loads:
        load.wait()
    third = []
    for s in range(sec_dev):
        arrived(second[s])
        inner = jnp.dot(psi_ref[s], comp[s], precision=PRECISE, preferred_element_type=jnp.float32)
        contrib[s] = jnp.dot(l_ref[s], inner, precision=PRECISE, preferred_element_type=jnp.float32)
        third.append(send(2, s, lambda p, s=s: contrib.at[s, rows_of(p, share_rows)], got_contrib.at[s, me]))
    for s in range(sec_dev):
        arrived(third[s])
        parts = [gathered(got_contrib, s, k) for k in range(n)]
        for c in range(channels):
            total = None
            for k in range(n):
                term = lax.rem(me + k, n)
                live = jnp.where(channel_ref[term] == c, pattern_ref[s, term], 0).astype(jnp.float32)
                total = live * parts[k] if total is None else total + live * parts[k]
            partial[s * channels + c] = total
    partial[sec_dev * channels] = jnp.zeros((share_rows, block_size), jnp.float32)
    for o in range(owners):
        for slot in range(capacity):
            at = o * capacity + slot
            outgoing[o, pl.ds(slot * share_rows, share_rows)] = partial[source_ref[at]]
    fourth = route(lambda p: outgoing.at[p], got_slots.at[here], route_sem, load_sem.at[3])
    for copies in (labels, fourth):
        arrived(copies)
    for copies in first + second + third + [labels, fourth]:
        for copy in copies[1:]:
            copy.wait_send()


def term_stage(rights, lefts, psi_blocks, couplings, pattern, channel, source, label_rows, channels):
    sec_dev, block_size, _ = psi_blocks.shape
    n = couplings.shape[0]
    owners = label_rows.shape[0]
    capacity = source.shape[0] // owners
    share_rows = block_size // n
    tiles = (sec_dev, n, share_rows, block_size)
    blocks = (sec_dev, block_size, block_size)
    routed = (owners, capacity * share_rows, block_size)
    hbm = pl.BlockSpec(memory_space=pl.ANY)
    smem = pl.BlockSpec(memory_space=pltpu.SMEM)
    vmem = pl.BlockSpec(memory_space=pltpu.VMEM)
    return pl.pallas_call(
        functools.partial(term_kernel, n, owners),
        out_shape=(
            jax.ShapeDtypeStruct(routed, jnp.float32),
            jax.ShapeDtypeStruct(label_rows.shape, jnp.float32),
        ),
        in_specs=[hbm, hbm, hbm, smem, smem, smem, smem, vmem],
        out_specs=(vmem, vmem),
        scratch_shapes=[
            pltpu.VMEM(blocks, jnp.float32),
            pltpu.VMEM(blocks, jnp.float32),
            pltpu.VMEM(tiles, jnp.float32),
            pltpu.VMEM(tiles, jnp.float32),
            pltpu.VMEM(blocks, jnp.float32),
            pltpu.VMEM(blocks, jnp.float32),
            pltpu.VMEM(tiles, jnp.float32),
            pltpu.VMEM((sec_dev * channels + 1, share_rows, block_size), jnp.float32),
            pltpu.VMEM(routed, jnp.float32),
            pltpu.SemaphoreType.DMA((3, sec_dev, n)),
            pltpu.SemaphoreType.DMA((3, sec_dev, n)),
            pltpu.SemaphoreType.DMA((3, sec_dev)),
            pltpu.SemaphoreType.DMA((4,)),
            pltpu.SemaphoreType.DMA((2, owners)),
            pltpu.SemaphoreType.DMA((2, owners)),
        ],
        compiler_params=pltpu.CompilerParams(collective_id=0, has_side_effects=True),
    )(rights, lefts, psi_blocks, couplings, pattern, channel, source, label_rows)


def slot_tables(target, owners):
    sec_dev, channels = target.shape
    slot_count = sec_dev * channels
    targets = target.reshape(slot_count)
    capacity = max(2, (slot_count + owners - 1) // owners)
    destination = targets // sec_dev
    slot_order = jnp.arange(slot_count, dtype=jnp.int32)
    earlier = (destination[None, :] == destination[:, None]) & (slot_order[None, :] < slot_order[:, None])
    position = destination * capacity + jnp.sum(earlier.astype(jnp.int32), axis=1)
    buffer_rows = jnp.arange(owners * capacity, dtype=jnp.int32)
    placing = buffer_rows[:, None] == position[None, :]
    keep = jnp.any(placing, axis=1)
    source = jnp.where(keep, jnp.sum(jnp.where(placing, slot_order[None, :], 0), axis=1), slot_count)
    labels = jnp.sum(jnp.where(placing, (targets % sec_dev + 1)[None, :], 0), axis=1).astype(jnp.float32)
    lanes = jnp.arange(128, dtype=jnp.int32)
    label_rows = jnp.where(lanes[None, None, :] == jnp.arange(capacity, dtype=jnp.int32)[None, :, None],
                           labels.reshape(owners, capacity)[:, :, None], 0.0)
    label_rows = jnp.sum(label_rows, axis=1, keepdims=True)
    return source.astype(jnp.int32), label_rows


def pick_arrivals(got_slots, got_labels, sec_dev, capacity):
    owners, rows, block_size = got_slots.shape
    share_rows = rows // capacity
    incoming = got_slots.reshape(owners, capacity, share_rows, block_size)
    in_labels = got_labels[:, 0, :capacity]
    local_ids = (jnp.arange(sec_dev, dtype=jnp.int32) + 1).astype(jnp.float32)
    picking = (in_labels[None, :, :] == local_ids[:, None, None]).astype(jnp.float32)
    return jnp.einsum("pos,osrk->prk", picking, incoming, precision=PRECISE)


def local(psi_blocks, left_ops, right_ops, couplings, pattern, channel, target):
    sec_dev, channels = target.shape
    owners = lax.axis_size("sector")
    source, label_rows = slot_tables(target, owners)
    got_slots, got_labels = term_stage(
        right_ops[0], left_ops[0], psi_blocks, couplings, pattern.T, channel, source, label_rows, channels
    )
    return pick_arrivals(got_slots, got_labels, sec_dev, source.shape[0] // owners)


def solution(mesh):
    placed = (
        P("sector", None, None),
        P("term", "sector", None, None),
        P("term", "sector", None, None),
        P(),
        P(None, "sector"),
        P(),
        P("sector", None),
    )
    return jax.shard_map(
        local, mesh=mesh, in_specs=placed, out_specs=P("sector", "term", None), check_vma=False
    )
```

```python
import functools

import jax
import jax.numpy as jnp
from jax import lax
from jax.experimental import pallas as pl
from jax.experimental.pallas import tpu as pltpu
from jax.sharding import PartitionSpec as P

MESH = pl.DeviceIdType.MESH

PRECISE = lax.Precision.HIGHEST


def rows_of(index, share_rows):
    return pl.ds(pl.multiple_of(index * share_rows, share_rows), share_rows)


def term_kernel(
    n, owners, r_ref, l_hbm, psi_hbm, coup_ref, pattern_ref, channel_ref, source_ref, label_ref,
    out_ref,
    got_slots, got_labels, l_ref, psi_ref, got_right, comp_rows, comp, contrib, got_contrib, partial, outgoing,
    send_sem, recv_sem, local_sem, load_sem, route_sem, label_sem,
):
    me = lax.axis_index("term")
    here = lax.axis_index("sector")
    sec_dev, _, share_rows, block_size = got_right.shape
    channels = (partial.shape[0] - 1) // sec_dev
    capacity = outgoing.shape[1] // share_rows
    barrier = pltpu.get_barrier_semaphore()
    for k in range(1, n):
        pl.semaphore_signal(barrier, inc=1, device_id={"term": lax.rem(me + k, n)}, device_id_type=MESH)
    for k in range(1, owners):
        pl.semaphore_signal(barrier, inc=1, device_id={"sector": lax.rem(here + k, owners)}, device_id_type=MESH)
    pl.semaphore_wait(barrier, n - 1 + owners - 1)

    def route(src_of, dst, sems, local):
        first = pltpu.make_async_copy(src_of(here), dst, local)
        first.start()
        copies = [first]
        for k in range(1, owners):
            peer = lax.rem(here + k, owners)
            copy = pltpu.make_async_remote_copy(
                src_ref=src_of(peer),
                dst_ref=dst,
                send_sem=sems.at[0, k],
                recv_sem=sems.at[1, k],
                device_id={"sector": peer},
                device_id_type=MESH,
            )
            copy.start()
            copies.append(copy)
        return copies

    labels = route(lambda p: label_ref.at[p], got_labels.at[here], label_sem, load_sem.at[2])

    def send(stage, s, src_of, dst):
        local = pltpu.make_async_copy(src_of(me), dst, local_sem.at[stage, s])
        local.start()
        copies = [local]
        for k in range(1, n):
            peer = lax.rem(me + k, n)
            copy = pltpu.make_async_remote_copy(
                src_ref=src_of(peer),
                dst_ref=dst,
                send_sem=send_sem.at[stage, s, k],
                recv_sem=recv_sem.at[stage, s, k],
                device_id={"term": peer},
                device_id_type=MESH,
            )
            copy.start()
            copies.append(copy)
        return copies

    def arrived(copies):
        copies[0].wait()
        for copy in copies[1:]:
            copy.wait_recv()

    def gathered(buf, s, k):
        return buf[s, lax.rem(me + k, n)]

    loads = [pltpu.make_async_copy(l_hbm, l_ref, load_sem.at[0]), pltpu.make_async_copy(psi_hbm, psi_ref, load_sem.at[1])]
    for load in loads:
        load.start()
    first = [send(0, s, lambda p, s=s: r_ref.at[s, rows_of(p, share_rows)], got_right.at[s, me]) for s in range(sec_dev)]
    second = []
    for s in range(sec_dev):
        arrived(first[s])
        parts = [gathered(got_right, s, k) for k in range(n)]
        for a in range(n):
            total = coup_ref[a, me] * parts[0]
            for k in range(1, n):
                total = total + coup_ref[a, lax.rem(me + k, n)] * parts[k]
            comp_rows[s, a] = total
        second.append(send(1, s, lambda p, s=s: comp_rows.at[s, p], comp.at[s, rows_of(me, share_rows)]))
    for load in loads:
        load.wait()
    third = []
    for s in range(sec_dev):
        arrived(second[s])
        inner = jnp.dot(psi_ref[s], comp[s], precision=PRECISE, preferred_element_type=jnp.float32)
        contrib[s] = jnp.dot(l_ref[s], inner, precision=PRECISE, preferred_element_type=jnp.float32)
        third.append(send(2, s, lambda p, s=s: contrib.at[s, rows_of(p, share_rows)], got_contrib.at[s, me]))
    for s in range(sec_dev):
        arrived(third[s])
        parts = [gathered(got_contrib, s, k) for k in range(n)]
        for c in range(channels):
            total = None
            for k in range(n):
                term = lax.rem(me + k, n)
                live = jnp.where(channel_ref[term] == c, pattern_ref[s, term], 0).astype(jnp.float32)
                total = live * parts[k] if total is None else total + live * parts[k]
            partial[s * channels + c] = total
    partial[sec_dev * channels] = jnp.zeros((share_rows, block_size), jnp.float32)
    for o in range(owners):
        for slot in range(capacity):
            at = o * capacity + slot
            outgoing[o, pl.ds(slot * share_rows, share_rows)] = partial[source_ref[at]]
    fourth = route(lambda p: outgoing.at[p], got_slots.at[here], route_sem, load_sem.at[3])
    for copies in (labels, fourth):
        arrived(copies)
    totals = [None] * sec_dev
    for o in range(owners):
        label_row = got_labels[o]
        for slot in range(capacity):
            label = jnp.broadcast_to(label_row[:, slot:slot + 1], (share_rows, block_size))
            rows = got_slots[o, pl.ds(slot * share_rows, share_rows)]
            for p in range(sec_dev):
                part = jnp.where(label == float(p + 1), rows, 0.0)
                totals[p] = part if totals[p] is None else totals[p] + part
    for p in range(sec_dev):
        out_ref[p] = totals[p]
    for copies in first + second + third + [labels, fourth]:
        for copy in copies[1:]:
            copy.wait_send()


def term_stage(rights, lefts, psi_blocks, couplings, pattern, channel, source, label_rows, channels):
    sec_dev, block_size, _ = psi_blocks.shape
    n = couplings.shape[0]
    owners = label_rows.shape[0]
    capacity = source.shape[0] // owners
    share_rows = block_size // n
    tiles = (sec_dev, n, share_rows, block_size)
    blocks = (sec_dev, block_size, block_size)
    routed = (owners, capacity * share_rows, block_size)
    hbm = pl.BlockSpec(memory_space=pl.ANY)
    smem = pl.BlockSpec(memory_space=pltpu.SMEM)
    vmem = pl.BlockSpec(memory_space=pltpu.VMEM)
    return pl.pallas_call(
        functools.partial(term_kernel, n, owners),
        out_shape=jax.ShapeDtypeStruct((sec_dev, share_rows, block_size), jnp.float32),
        in_specs=[hbm, hbm, hbm, smem, smem, smem, smem, vmem],
        out_specs=vmem,
        scratch_shapes=[
            pltpu.VMEM(routed, jnp.float32),
            pltpu.VMEM(label_rows.shape, jnp.float32),
            pltpu.VMEM(blocks, jnp.float32),
            pltpu.VMEM(blocks, jnp.float32),
            pltpu.VMEM(tiles, jnp.float32),
            pltpu.VMEM(tiles, jnp.float32),
            pltpu.VMEM(blocks, jnp.float32),
            pltpu.VMEM(blocks, jnp.float32),
            pltpu.VMEM(tiles, jnp.float32),
            pltpu.VMEM((sec_dev * channels + 1, share_rows, block_size), jnp.float32),
            pltpu.VMEM(routed, jnp.float32),
            pltpu.SemaphoreType.DMA((3, sec_dev, n)),
            pltpu.SemaphoreType.DMA((3, sec_dev, n)),
            pltpu.SemaphoreType.DMA((3, sec_dev)),
            pltpu.SemaphoreType.DMA((4,)),
            pltpu.SemaphoreType.DMA((2, owners)),
            pltpu.SemaphoreType.DMA((2, owners)),
        ],
        compiler_params=pltpu.CompilerParams(collective_id=0, has_side_effects=True),
    )(rights, lefts, psi_blocks, couplings, pattern, channel, source, label_rows)


def slot_tables(target, owners):
    sec_dev, channels = target.shape
    slot_count = sec_dev * channels
    targets = target.reshape(slot_count)
    capacity = max(2, (slot_count + owners - 1) // owners)
    destination = targets // sec_dev
    slot_order = jnp.arange(slot_count, dtype=jnp.int32)
    earlier = (destination[None, :] == destination[:, None]) & (slot_order[None, :] < slot_order[:, None])
    position = destination * capacity + jnp.sum(earlier.astype(jnp.int32), axis=1)
    buffer_rows = jnp.arange(owners * capacity, dtype=jnp.int32)
    placing = buffer_rows[:, None] == position[None, :]
    keep = jnp.any(placing, axis=1)
    source = jnp.where(keep, jnp.sum(jnp.where(placing, slot_order[None, :], 0), axis=1), slot_count)
    labels = jnp.sum(jnp.where(placing, (targets % sec_dev + 1)[None, :], 0), axis=1).astype(jnp.float32)
    lanes = jnp.arange(128, dtype=jnp.int32)
    label_rows = jnp.where(lanes[None, None, :] == jnp.arange(capacity, dtype=jnp.int32)[None, :, None],
                           labels.reshape(owners, capacity)[:, :, None], 0.0)
    label_rows = jnp.sum(label_rows, axis=1, keepdims=True)
    return source.astype(jnp.int32), label_rows


def local(psi_blocks, left_ops, right_ops, couplings, pattern, channel, target):
    sec_dev, channels = target.shape
    owners = lax.axis_size("sector")
    source, label_rows = slot_tables(target, owners)
    return term_stage(
        right_ops[0], left_ops[0], psi_blocks, couplings, pattern.T, channel, source, label_rows, channels
    )


def solution(mesh):
    placed = (
        P("sector", None, None),
        P("term", "sector", None, None),
        P("term", "sector", None, None),
        P(),
        P(None, "sector"),
        P(),
        P("sector", None),
    )
    return jax.shard_map(
        local, mesh=mesh, in_specs=placed, out_specs=P("sector", "term", None), check_vma=False
    )
```

```python
import functools

import jax
import jax.numpy as jnp
from jax import lax
from jax.experimental import pallas as pl
from jax.experimental.pallas import tpu as pltpu
from jax.sharding import PartitionSpec as P

MESH = pl.DeviceIdType.MESH

PRECISE = lax.Precision.HIGHEST


def rows_of(index, share_rows):
    return pl.ds(pl.multiple_of(index * share_rows, share_rows), share_rows)


def term_kernel(
    n, owners, r_ref, l_hbm, psi_hbm, coup_ref, pattern_ref, channel_ref, source_ref, label_ref,
    out_ref,
    got_slots, got_labels, l_ref, psi_ref, got_right, comp_rows, comp, contrib, got_contrib, partial, outgoing,
    send_sem, recv_sem, local_sem, load_sem, route_sem, label_sem,
):
    me = lax.axis_index("term")
    here = lax.axis_index("sector")
    sec_dev, _, share_rows, block_size = got_right.shape
    channels = (partial.shape[0] - 1) // sec_dev
    capacity = outgoing.shape[2] // (share_rows // 2)
    barrier = pltpu.get_barrier_semaphore()
    for k in range(1, n):
        pl.semaphore_signal(barrier, inc=1, device_id={"term": lax.rem(me + k, n)}, device_id_type=MESH)
    for k in range(1, owners):
        pl.semaphore_signal(barrier, inc=1, device_id={"sector": lax.rem(here + k, owners)}, device_id_type=MESH)
    pl.semaphore_wait(barrier, n - 1 + owners - 1)

    def route(src_of, dst, sems, local):
        first = pltpu.make_async_copy(src_of(here), dst, local)
        first.start()
        copies = [first]
        for k in range(1, owners):
            peer = lax.rem(here + k, owners)
            copy = pltpu.make_async_remote_copy(
                src_ref=src_of(peer),
                dst_ref=dst,
                send_sem=sems.at[0, k],
                recv_sem=sems.at[1, k],
                device_id={"sector": peer},
                device_id_type=MESH,
            )
            copy.start()
            copies.append(copy)
        return copies

    labels = route(lambda p: label_ref.at[p], got_labels.at[here], label_sem, load_sem.at[2])

    def send(stage, s, src_of, dst):
        local = pltpu.make_async_copy(src_of(me), dst, local_sem.at[stage, s])
        local.start()
        copies = [local]
        for k in range(1, n):
            peer = lax.rem(me + k, n)
            copy = pltpu.make_async_remote_copy(
                src_ref=src_of(peer),
                dst_ref=dst,
                send_sem=send_sem.at[stage, s, k],
                recv_sem=recv_sem.at[stage, s, k],
                device_id={"term": peer},
                device_id_type=MESH,
            )
            copy.start()
            copies.append(copy)
        return copies

    def arrived(copies):
        copies[0].wait()
        for copy in copies[1:]:
            copy.wait_recv()

    def gathered(buf, s, k):
        return buf[s, lax.rem(me + k, n)]

    loads = [pltpu.make_async_copy(l_hbm, l_ref, load_sem.at[0]), pltpu.make_async_copy(psi_hbm, psi_ref, load_sem.at[1])]
    for load in loads:
        load.start()
    first = [send(0, s, lambda p, s=s: r_ref.at[s, rows_of(p, share_rows)], got_right.at[s, me]) for s in range(sec_dev)]
    second = []
    for s in range(sec_dev):
        arrived(first[s])
        parts = [gathered(got_right, s, k) for k in range(n)]
        for a in range(n):
            total = coup_ref[a, me] * parts[0]
            for k in range(1, n):
                total = total + coup_ref[a, lax.rem(me + k, n)] * parts[k]
            comp_rows[s, a] = total
        second.append(send(1, s, lambda p, s=s: comp_rows.at[s, p], comp.at[s, rows_of(me, share_rows)]))
    for load in loads:
        load.wait()
    half = share_rows // 2
    third = [[], []]
    for s in range(sec_dev):
        arrived(second[s])
        inner = jnp.dot(psi_ref[s], comp[s], precision=PRECISE, preferred_element_type=jnp.float32)
        contrib[s] = jnp.dot(l_ref[s], inner, precision=PRECISE, preferred_element_type=jnp.float32)
        third[0].append(send(2, s, lambda p, s=s: contrib.at[s, pl.ds(p * share_rows, half)], got_contrib.at[s, me, pl.ds(0, half)]))
    for s in range(sec_dev):
        third[1].append(send(3, s, lambda p, s=s: contrib.at[s, pl.ds(p * share_rows + half, half)], got_contrib.at[s, me, pl.ds(half, half)]))
    partial[sec_dev * channels] = jnp.zeros((share_rows, block_size), jnp.float32)
    fourth = []
    for h in range(2):
        rows_h = pl.ds(h * half, half)
        for s in range(sec_dev):
            arrived(third[h][s])
            parts = [got_contrib[s, lax.rem(me + k, n), rows_h] for k in range(n)]
            for c in range(channels):
                total = None
                for k in range(n):
                    term = lax.rem(me + k, n)
                    live = jnp.where(channel_ref[term] == c, pattern_ref[s, term], 0).astype(jnp.float32)
                    total = live * parts[k] if total is None else total + live * parts[k]
                partial[s * channels + c, rows_h] = total
        for o in range(owners):
            for slot in range(capacity):
                at = o * capacity + slot
                outgoing[h, o, pl.ds(slot * half, half)] = partial[source_ref[at], rows_h]
        fourth.append(route(lambda p, h=h: outgoing.at[h, p], got_slots.at[h, here], route_sem.at[h], load_sem.at[3 + h]))
    arrived(labels)
    for h in range(2):
        arrived(fourth[h])
        totals = [None] * sec_dev
        for o in range(owners):
            label_row = got_labels[o]
            for slot in range(capacity):
                label = jnp.broadcast_to(label_row[:, slot:slot + 1], (half, block_size))
                rows = got_slots[h, o, pl.ds(slot * half, half)]
                for p in range(sec_dev):
                    part = jnp.where(label == float(p + 1), rows, 0.0)
                    totals[p] = part if totals[p] is None else totals[p] + part
        for p in range(sec_dev):
            out_ref[p, pl.ds(h * half, half)] = totals[p]
    for copies in first + second + third[0] + third[1] + [labels] + fourth:
        for copy in copies[1:]:
            copy.wait_send()


def term_stage(rights, lefts, psi_blocks, couplings, pattern, channel, source, label_rows, channels):
    sec_dev, block_size, _ = psi_blocks.shape
    n = couplings.shape[0]
    owners = label_rows.shape[0]
    capacity = source.shape[0] // owners
    share_rows = block_size // n
    tiles = (sec_dev, n, share_rows, block_size)
    blocks = (sec_dev, block_size, block_size)
    routed = (owners, capacity * share_rows // 2, block_size)
    hbm = pl.BlockSpec(memory_space=pl.ANY)
    smem = pl.BlockSpec(memory_space=pltpu.SMEM)
    vmem = pl.BlockSpec(memory_space=pltpu.VMEM)
    return pl.pallas_call(
        functools.partial(term_kernel, n, owners),
        out_shape=jax.ShapeDtypeStruct((sec_dev, share_rows, block_size), jnp.float32),
        in_specs=[hbm, hbm, hbm, smem, smem, smem, smem, vmem],
        out_specs=vmem,
        scratch_shapes=[
            pltpu.VMEM((2,) + routed, jnp.float32),
            pltpu.VMEM(label_rows.shape, jnp.float32),
            pltpu.VMEM(blocks, jnp.float32),
            pltpu.VMEM(blocks, jnp.float32),
            pltpu.VMEM(tiles, jnp.float32),
            pltpu.VMEM(tiles, jnp.float32),
            pltpu.VMEM(blocks, jnp.float32),
            pltpu.VMEM(blocks, jnp.float32),
            pltpu.VMEM(tiles, jnp.float32),
            pltpu.VMEM((sec_dev * channels + 1, share_rows, block_size), jnp.float32),
            pltpu.VMEM((2,) + routed, jnp.float32),
            pltpu.SemaphoreType.DMA((4, sec_dev, n)),
            pltpu.SemaphoreType.DMA((4, sec_dev, n)),
            pltpu.SemaphoreType.DMA((4, sec_dev)),
            pltpu.SemaphoreType.DMA((5,)),
            pltpu.SemaphoreType.DMA((2, 2, owners)),
            pltpu.SemaphoreType.DMA((2, owners)),
        ],
        compiler_params=pltpu.CompilerParams(collective_id=0, has_side_effects=True),
    )(rights, lefts, psi_blocks, couplings, pattern, channel, source, label_rows)


def slot_tables(target, owners):
    sec_dev, channels = target.shape
    slot_count = sec_dev * channels
    targets = target.reshape(slot_count)
    capacity = max(2, (slot_count + owners - 1) // owners)
    destination = targets // sec_dev
    slot_order = jnp.arange(slot_count, dtype=jnp.int32)
    earlier = (destination[None, :] == destination[:, None]) & (slot_order[None, :] < slot_order[:, None])
    position = destination * capacity + jnp.sum(earlier.astype(jnp.int32), axis=1)
    buffer_rows = jnp.arange(owners * capacity, dtype=jnp.int32)
    placing = buffer_rows[:, None] == position[None, :]
    keep = jnp.any(placing, axis=1)
    source = jnp.where(keep, jnp.sum(jnp.where(placing, slot_order[None, :], 0), axis=1), slot_count)
    labels = jnp.sum(jnp.where(placing, (targets % sec_dev + 1)[None, :], 0), axis=1).astype(jnp.float32)
    lanes = jnp.arange(128, dtype=jnp.int32)
    label_rows = jnp.where(lanes[None, None, :] == jnp.arange(capacity, dtype=jnp.int32)[None, :, None],
                           labels.reshape(owners, capacity)[:, :, None], 0.0)
    label_rows = jnp.sum(label_rows, axis=1, keepdims=True)
    return source.astype(jnp.int32), label_rows


def local(psi_blocks, left_ops, right_ops, couplings, pattern, channel, target):
    sec_dev, channels = target.shape
    owners = lax.axis_size("sector")
    source, label_rows = slot_tables(target, owners)
    return term_stage(
        right_ops[0], left_ops[0], psi_blocks, couplings, pattern.T, channel, source, label_rows, channels
    )


def solution(mesh):
    placed = (
        P("sector", None, None),
        P("term", "sector", None, None),
        P("term", "sector", None, None),
        P(),
        P(None, "sector"),
        P(),
        P("sector", None),
    )
    return jax.shard_map(
        local, mesh=mesh, in_specs=placed, out_specs=P("sector", "term", None), check_vma=False
    )
```

```python
import functools

import jax
import jax.numpy as jnp
from jax import lax
from jax.experimental import pallas as pl
from jax.experimental.pallas import tpu as pltpu
from jax.sharding import PartitionSpec as P

MESH = pl.DeviceIdType.MESH

PRECISE = lax.Precision.HIGHEST


def rows_of(index, share_rows):
    return pl.ds(pl.multiple_of(index * share_rows, share_rows), share_rows)


def term_kernel(
    n, owners, r_ref, l_hbm, psi_hbm, coup_ref, pattern_ref, channel_ref, target_ref,
    out_ref,
    got_slots, got_labels, label_rows, key_tab, label_tab, source_tab, slot_label, l_ref, psi_ref, got_right, comp_rows, comp, contrib, got_contrib, partial, outgoing,
    send_sem, recv_sem, local_sem, load_sem, route_sem, label_sem,
):
    me = lax.axis_index("term")
    here = lax.axis_index("sector")
    sec_dev, _, share_rows, block_size = got_right.shape
    channels = (partial.shape[0] - 1) // sec_dev
    capacity = outgoing.shape[1] // share_rows
    barrier = pltpu.get_barrier_semaphore()
    for k in range(1, n):
        pl.semaphore_signal(barrier, inc=1, device_id={"term": lax.rem(me + k, n)}, device_id_type=MESH)
    for k in range(1, owners):
        pl.semaphore_signal(barrier, inc=1, device_id={"sector": lax.rem(here + k, owners)}, device_id_type=MESH)
    pl.semaphore_wait(barrier, n - 1 + owners - 1)

    def route(src_of, dst, sems, local):
        first = pltpu.make_async_copy(src_of(here), dst, local)
        first.start()
        copies = [first]
        for k in range(1, owners):
            peer = lax.rem(here + k, owners)
            copy = pltpu.make_async_remote_copy(
                src_ref=src_of(peer),
                dst_ref=dst,
                send_sem=sems.at[0, k],
                recv_sem=sems.at[1, k],
                device_id={"sector": peer},
                device_id_type=MESH,
            )
            copy.start()
            copies.append(copy)
        return copies


    def send(stage, s, src_of, dst):
        local = pltpu.make_async_copy(src_of(me), dst, local_sem.at[stage, s])
        local.start()
        copies = [local]
        for k in range(1, n):
            peer = lax.rem(me + k, n)
            copy = pltpu.make_async_remote_copy(
                src_ref=src_of(peer),
                dst_ref=dst,
                send_sem=send_sem.at[stage, s, k],
                recv_sem=recv_sem.at[stage, s, k],
                device_id={"term": peer},
                device_id_type=MESH,
            )
            copy.start()
            copies.append(copy)
        return copies

    def arrived(copies):
        copies[0].wait()
        for copy in copies[1:]:
            copy.wait_recv()

    def gathered(buf, s, k):
        return buf[s, lax.rem(me + k, n)]

    loads = [pltpu.make_async_copy(l_hbm, l_ref, load_sem.at[0]), pltpu.make_async_copy(psi_hbm, psi_ref, load_sem.at[1])]
    for load in loads:
        load.start()
    first = [send(0, s, lambda p, s=s: r_ref.at[s, rows_of(p, share_rows)], got_right.at[s, me]) for s in range(sec_dev)]
    slot_count = sec_dev * channels
    owner_of = [target_ref[i // channels, i % channels] // sec_dev for i in range(slot_count)]
    for i in range(slot_count):
        rank = 0
        for j in range(i):
            rank = rank + jnp.where(owner_of[j] == owner_of[i], 1, 0)
        key_tab[i] = owner_of[i] * capacity + rank
        label_tab[i] = (target_ref[i // channels, i % channels] % sec_dev + 1).astype(jnp.float32)

    def fill_row(q, carry):
        found = jnp.int32(slot_count)
        label = jnp.float32(0.0)
        for i in range(slot_count):
            hit = key_tab[i] == q
            found = jnp.where(hit, i, found)
            label = jnp.where(hit, label_tab[i], label)
        source_tab[q] = found
        slot_label[q] = label
        return carry

    lax.fori_loop(0, owners * capacity, fill_row, 0)
    lanes = lax.broadcasted_iota(jnp.int32, (1, block_size), 1)

    def fill_labels(o, carry):
        row = jnp.zeros((1, block_size), jnp.float32)
        for slot in range(capacity):
            row = jnp.where(lanes == slot, slot_label[o * capacity + slot], row)
        label_rows[o] = row
        return carry

    lax.fori_loop(0, owners, fill_labels, 0)
    labels = route(lambda p: label_rows.at[p], got_labels.at[here], label_sem, load_sem.at[2])

    second = []
    for s in range(sec_dev):
        arrived(first[s])
        parts = [gathered(got_right, s, k) for k in range(n)]
        for a in range(n):
            total = coup_ref[a, me] * parts[0]
            for k in range(1, n):
                total = total + coup_ref[a, lax.rem(me + k, n)] * parts[k]
            comp_rows[s, a] = total
        second.append(send(1, s, lambda p, s=s: comp_rows.at[s, p], comp.at[s, rows_of(me, share_rows)]))
    for load in loads:
        load.wait()
    third = []
    for s in range(sec_dev):
        arrived(second[s])
        inner = jnp.dot(psi_ref[s], comp[s], precision=PRECISE, preferred_element_type=jnp.float32)
        contrib[s] = jnp.dot(l_ref[s], inner, precision=PRECISE, preferred_element_type=jnp.float32)
        third.append(send(2, s, lambda p, s=s: contrib.at[s, rows_of(p, share_rows)], got_contrib.at[s, me]))
    for s in range(sec_dev):
        arrived(third[s])
        parts = [gathered(got_contrib, s, k) for k in range(n)]
        for c in range(channels):
            total = None
            for k in range(n):
                term = lax.rem(me + k, n)
                live = jnp.where(channel_ref[term] == c, pattern_ref[s, term], 0).astype(jnp.float32)
                total = live * parts[k] if total is None else total + live * parts[k]
            partial[s * channels + c] = total
    partial[sec_dev * channels] = jnp.zeros((share_rows, block_size), jnp.float32)
    for o in range(owners):
        for slot in range(capacity):
            at = o * capacity + slot
            outgoing[o, pl.ds(slot * share_rows, share_rows)] = partial[source_tab[at]]
    fourth = route(lambda p: outgoing.at[p], got_slots.at[here], route_sem, load_sem.at[3])
    for copies in (labels, fourth):
        arrived(copies)
    totals = [None] * sec_dev
    for o in range(owners):
        label_row = got_labels[o]
        for slot in range(capacity):
            label = jnp.broadcast_to(label_row[:, slot:slot + 1], (share_rows, block_size))
            rows = got_slots[o, pl.ds(slot * share_rows, share_rows)]
            for p in range(sec_dev):
                part = jnp.where(label == float(p + 1), rows, 0.0)
                totals[p] = part if totals[p] is None else totals[p] + part
    for p in range(sec_dev):
        out_ref[p] = totals[p]
    for copies in first + second + third + [labels, fourth]:
        for copy in copies[1:]:
            copy.wait_send()


def term_stage(rights, lefts, psi_blocks, couplings, pattern, channel, target, owners):
    sec_dev, block_size, _ = psi_blocks.shape
    n = couplings.shape[0]
    channels = target.shape[1]
    capacity = max(2, (sec_dev * channels + owners - 1) // owners)
    share_rows = block_size // n
    tiles = (sec_dev, n, share_rows, block_size)
    blocks = (sec_dev, block_size, block_size)
    routed = (owners, capacity * share_rows, block_size)
    hbm = pl.BlockSpec(memory_space=pl.ANY)
    smem = pl.BlockSpec(memory_space=pltpu.SMEM)
    vmem = pl.BlockSpec(memory_space=pltpu.VMEM)
    return pl.pallas_call(
        functools.partial(term_kernel, n, owners),
        out_shape=jax.ShapeDtypeStruct((sec_dev, share_rows, block_size), jnp.float32),
        in_specs=[hbm, hbm, hbm, smem, smem, smem, smem],
        out_specs=vmem,
        scratch_shapes=[
            pltpu.VMEM(routed, jnp.float32),
            pltpu.VMEM((owners, 1, block_size), jnp.float32),
            pltpu.VMEM((owners, 1, block_size), jnp.float32),
            pltpu.SMEM((sec_dev * channels,), jnp.int32),
            pltpu.SMEM((sec_dev * channels,), jnp.float32),
            pltpu.SMEM((owners * capacity,), jnp.int32),
            pltpu.SMEM((owners * capacity,), jnp.float32),
            pltpu.VMEM(blocks, jnp.float32),
            pltpu.VMEM(blocks, jnp.float32),
            pltpu.VMEM(tiles, jnp.float32),
            pltpu.VMEM(tiles, jnp.float32),
            pltpu.VMEM(blocks, jnp.float32),
            pltpu.VMEM(blocks, jnp.float32),
            pltpu.VMEM(tiles, jnp.float32),
            pltpu.VMEM((sec_dev * channels + 1, share_rows, block_size), jnp.float32),
            pltpu.VMEM(routed, jnp.float32),
            pltpu.SemaphoreType.DMA((3, sec_dev, n)),
            pltpu.SemaphoreType.DMA((3, sec_dev, n)),
            pltpu.SemaphoreType.DMA((3, sec_dev)),
            pltpu.SemaphoreType.DMA((4,)),
            pltpu.SemaphoreType.DMA((2, owners)),
            pltpu.SemaphoreType.DMA((2, owners)),
        ],
        compiler_params=pltpu.CompilerParams(collective_id=0, has_side_effects=True),
    )(rights, lefts, psi_blocks, couplings, pattern, channel, target)


def local(psi_blocks, left_ops, right_ops, couplings, pattern, channel, target):
    owners = lax.axis_size("sector")
    return term_stage(right_ops[0], left_ops[0], psi_blocks, couplings, pattern.T, channel, target, owners)


def solution(mesh):
    placed = (
        P("sector", None, None),
        P("term", "sector", None, None),
        P("term", "sector", None, None),
        P(),
        P(None, "sector"),
        P(),
        P("sector", None),
    )
    return jax.shard_map(
        local, mesh=mesh, in_specs=placed, out_specs=P("sector", "term", None), check_vma=False
    )
```

```python
import functools

import jax
import jax.numpy as jnp
from jax import lax
from jax.experimental import pallas as pl
from jax.experimental.pallas import tpu as pltpu
from jax.sharding import PartitionSpec as P

MESH = pl.DeviceIdType.MESH

PRECISE = lax.Precision.HIGHEST


def rows_of(index, share_rows):
    return pl.ds(pl.multiple_of(index * share_rows, share_rows), share_rows)


def term_kernel(
    n, owners, r_ref, l_hbm, psi_hbm, coup_ref, pattern_ref, channel_ref, target_ref,
    out_ref,
    got_slots, got_labels, label_rows, key_tab, label_tab, source_tab, slot_label, l_ref, psi_ref, got_right, comp_rows, comp, contrib, got_contrib, partial, outgoing,
    send_sem, recv_sem, local_sem, load_sem, route_sem, label_sem,
):
    me = lax.axis_index("term")
    here = lax.axis_index("sector")
    sec_dev, _, share_rows, block_size = got_right.shape
    channels = (partial.shape[0] - 1) // sec_dev
    capacity = outgoing.shape[1] // share_rows
    loads = [pltpu.make_async_copy(l_hbm, l_ref, load_sem.at[0]), pltpu.make_async_copy(psi_hbm, psi_ref, load_sem.at[1])]
    for load in loads:
        load.start()
    barrier = pltpu.get_barrier_semaphore()
    for k in range(1, n):
        pl.semaphore_signal(barrier, inc=1, device_id={"term": lax.rem(me + k, n)}, device_id_type=MESH)
    for k in range(1, owners):
        pl.semaphore_signal(barrier, inc=1, device_id={"sector": lax.rem(here + k, owners)}, device_id_type=MESH)
    pl.semaphore_wait(barrier, n - 1 + owners - 1)

    def route(src_of, dst, sems, local):
        first = pltpu.make_async_copy(src_of(here), dst, local)
        first.start()
        copies = [first]
        for k in range(1, owners):
            peer = lax.rem(here + k, owners)
            copy = pltpu.make_async_remote_copy(
                src_ref=src_of(peer),
                dst_ref=dst,
                send_sem=sems.at[0, k],
                recv_sem=sems.at[1, k],
                device_id={"sector": peer},
                device_id_type=MESH,
            )
            copy.start()
            copies.append(copy)
        return copies


    def send(stage, s, src_of, dst):
        local = pltpu.make_async_copy(src_of(me), dst, local_sem.at[stage, s])
        local.start()
        copies = [local]
        for k in range(1, n):
            peer = lax.rem(me + k, n)
            copy = pltpu.make_async_remote_copy(
                src_ref=src_of(peer),
                dst_ref=dst,
                send_sem=send_sem.at[stage, s, k],
                recv_sem=recv_sem.at[stage, s, k],
                device_id={"term": peer},
                device_id_type=MESH,
            )
            copy.start()
            copies.append(copy)
        return copies

    def arrived(copies):
        copies[0].wait()
        for copy in copies[1:]:
            copy.wait_recv()

    def gathered(buf, s, k):
        return buf[s, lax.rem(me + k, n)]

    first = [send(0, s, lambda p, s=s: r_ref.at[s, rows_of(p, share_rows)], got_right.at[s, me]) for s in range(sec_dev)]
    slot_count = sec_dev * channels
    owner_of = [target_ref[i // channels, i % channels] // sec_dev for i in range(slot_count)]
    for i in range(slot_count):
        rank = 0
        for j in range(i):
            rank = rank + jnp.where(owner_of[j] == owner_of[i], 1, 0)
        key_tab[i] = owner_of[i] * capacity + rank
        label_tab[i] = (target_ref[i // channels, i % channels] % sec_dev + 1).astype(jnp.float32)

    def fill_row(q, carry):
        found = jnp.int32(slot_count)
        label = jnp.float32(0.0)
        for i in range(slot_count):
            hit = key_tab[i] == q
            found = jnp.where(hit, i, found)
            label = jnp.where(hit, label_tab[i], label)
        source_tab[q] = found
        slot_label[q] = label
        return carry

    lax.fori_loop(0, owners * capacity, fill_row, 0)
    lanes = lax.broadcasted_iota(jnp.int32, (1, block_size), 1)

    def fill_labels(o, carry):
        row = jnp.zeros((1, block_size), jnp.float32)
        for slot in range(capacity):
            row = jnp.where(lanes == slot, slot_label[o * capacity + slot], row)
        label_rows[o] = row
        return carry

    lax.fori_loop(0, owners, fill_labels, 0)
    labels = route(lambda p: label_rows.at[p], got_labels.at[here], label_sem, load_sem.at[2])
    for load in loads:
        load.wait()
    for s in range(sec_dev):
        l_ref[s] = jnp.dot(l_ref[s], psi_ref[s], precision=PRECISE, preferred_element_type=jnp.float32)

    second = []
    for s in range(sec_dev):
        arrived(first[s])
        parts = [gathered(got_right, s, k) for k in range(n)]
        for a in range(n):
            total = coup_ref[a, me] * parts[0]
            for k in range(1, n):
                total = total + coup_ref[a, lax.rem(me + k, n)] * parts[k]
            comp_rows[s, a] = total
        second.append(send(1, s, lambda p, s=s: comp_rows.at[s, p], comp.at[s, rows_of(me, share_rows)]))
    third = []
    for s in range(sec_dev):
        arrived(second[s])
        contrib[s] = jnp.dot(l_ref[s], comp[s], precision=PRECISE, preferred_element_type=jnp.float32)
        third.append(send(2, s, lambda p, s=s: contrib.at[s, rows_of(p, share_rows)], got_contrib.at[s, me]))
    for s in range(sec_dev):
        arrived(third[s])
        parts = [gathered(got_contrib, s, k) for k in range(n)]
        for c in range(channels):
            total = None
            for k in range(n):
                term = lax.rem(me + k, n)
                live = jnp.where(channel_ref[term] == c, pattern_ref[s, term], 0).astype(jnp.float32)
                total = live * parts[k] if total is None else total + live * parts[k]
            partial[s * channels + c] = total
    partial[sec_dev * channels] = jnp.zeros((share_rows, block_size), jnp.float32)
    for o in range(owners):
        for slot in range(capacity):
            at = o * capacity + slot
            outgoing[o, pl.ds(slot * share_rows, share_rows)] = partial[source_tab[at]]
    fourth = route(lambda p: outgoing.at[p], got_slots.at[here], route_sem, load_sem.at[3])
    for copies in (labels, fourth):
        arrived(copies)
    totals = [None] * sec_dev
    for o in range(owners):
        label_row = got_labels[o]
        for slot in range(capacity):
            label = jnp.broadcast_to(label_row[:, slot:slot + 1], (share_rows, block_size))
            rows = got_slots[o, pl.ds(slot * share_rows, share_rows)]
            for p in range(sec_dev):
                part = jnp.where(label == float(p + 1), rows, 0.0)
                totals[p] = part if totals[p] is None else totals[p] + part
    for p in range(sec_dev):
        out_ref[p] = totals[p]
    for copies in first + second + third + [labels, fourth]:
        for copy in copies[1:]:
            copy.wait_send()


def term_stage(rights, lefts, psi_blocks, couplings, pattern, channel, target, owners):
    sec_dev, block_size, _ = psi_blocks.shape
    n = couplings.shape[0]
    channels = target.shape[1]
    capacity = max(2, (sec_dev * channels + owners - 1) // owners)
    share_rows = block_size // n
    tiles = (sec_dev, n, share_rows, block_size)
    blocks = (sec_dev, block_size, block_size)
    routed = (owners, capacity * share_rows, block_size)
    hbm = pl.BlockSpec(memory_space=pl.ANY)
    smem = pl.BlockSpec(memory_space=pltpu.SMEM)
    vmem = pl.BlockSpec(memory_space=pltpu.VMEM)
    return pl.pallas_call(
        functools.partial(term_kernel, n, owners),
        out_shape=jax.ShapeDtypeStruct((sec_dev, share_rows, block_size), jnp.float32),
        in_specs=[hbm, hbm, hbm, smem, smem, smem, smem],
        out_specs=vmem,
        scratch_shapes=[
            pltpu.VMEM(routed, jnp.float32),
            pltpu.VMEM((owners, 1, block_size), jnp.float32),
            pltpu.VMEM((owners, 1, block_size), jnp.float32),
            pltpu.SMEM((sec_dev * channels,), jnp.int32),
            pltpu.SMEM((sec_dev * channels,), jnp.float32),
            pltpu.SMEM((owners * capacity,), jnp.int32),
            pltpu.SMEM((owners * capacity,), jnp.float32),
            pltpu.VMEM(blocks, jnp.float32),
            pltpu.VMEM(blocks, jnp.float32),
            pltpu.VMEM(tiles, jnp.float32),
            pltpu.VMEM(tiles, jnp.float32),
            pltpu.VMEM(blocks, jnp.float32),
            pltpu.VMEM(blocks, jnp.float32),
            pltpu.VMEM(tiles, jnp.float32),
            pltpu.VMEM((sec_dev * channels + 1, share_rows, block_size), jnp.float32),
            pltpu.VMEM(routed, jnp.float32),
            pltpu.SemaphoreType.DMA((3, sec_dev, n)),
            pltpu.SemaphoreType.DMA((3, sec_dev, n)),
            pltpu.SemaphoreType.DMA((3, sec_dev)),
            pltpu.SemaphoreType.DMA((4,)),
            pltpu.SemaphoreType.DMA((2, owners)),
            pltpu.SemaphoreType.DMA((2, owners)),
        ],
        compiler_params=pltpu.CompilerParams(collective_id=0, has_side_effects=True),
    )(rights, lefts, psi_blocks, couplings, pattern, channel, target)


def local(psi_blocks, left_ops, right_ops, couplings, pattern, channel, target):
    owners = lax.axis_size("sector")
    return term_stage(right_ops[0], left_ops[0], psi_blocks, couplings, pattern.T, channel, target, owners)


def solution(mesh):
    placed = (
        P("sector", None, None),
        P("term", "sector", None, None),
        P("term", "sector", None, None),
        P(),
        P(None, "sector"),
        P(),
        P("sector", None),
    )
    return jax.shard_map(
        local, mesh=mesh, in_specs=placed, out_specs=P("sector", "term", None), check_vma=False
    )
```

```python
import functools

import jax
import jax.numpy as jnp
from jax import lax
from jax.experimental import pallas as pl
from jax.experimental.pallas import tpu as pltpu
from jax.sharding import PartitionSpec as P

MESH = pl.DeviceIdType.MESH

PRECISE = lax.Precision.HIGHEST


def rows_of(index, share_rows):
    return pl.ds(pl.multiple_of(index * share_rows, share_rows), share_rows)


def term_kernel(
    n, owners, r_ref, l_hbm, psi_hbm, coup_ref, pattern_ref, channel_ref, target_ref,
    out_ref,
    got_slots, got_labels, label_rows, key_tab, label_tab, source_tab, slot_label, l_ref, psi_ref, got_right, comp_rows, comp, contrib, got_contrib, partial, outgoing,
    send_sem, recv_sem, local_sem, load_sem, route_sem, label_sem,
):
    me = lax.axis_index("term")
    here = lax.axis_index("sector")
    sec_dev, _, share_rows, block_size = got_right.shape
    channels = (partial.shape[0] - 1) // sec_dev
    capacity = outgoing.shape[1] // share_rows
    loads = [pltpu.make_async_copy(l_hbm, l_ref, load_sem.at[0]), pltpu.make_async_copy(psi_hbm, psi_ref, load_sem.at[1])]
    for load in loads:
        load.start()
    barrier = pltpu.get_barrier_semaphore()
    for k in range(1, n):
        pl.semaphore_signal(barrier, inc=1, device_id={"term": lax.rem(me + k, n)}, device_id_type=MESH)
    for k in range(1, owners):
        pl.semaphore_signal(barrier, inc=1, device_id={"sector": lax.rem(here + k, owners)}, device_id_type=MESH)
    pl.semaphore_wait(barrier, n - 1 + owners - 1)

    def route(src_of, dst, sems, local):
        first = pltpu.make_async_copy(src_of(here), dst, local)
        first.start()
        copies = [first]
        for k in range(1, owners):
            peer = lax.rem(here + k, owners)
            copy = pltpu.make_async_remote_copy(
                src_ref=src_of(peer),
                dst_ref=dst,
                send_sem=sems.at[0, k],
                recv_sem=sems.at[1, k],
                device_id={"sector": peer},
                device_id_type=MESH,
            )
            copy.start()
            copies.append(copy)
        return copies


    def send(stage, s, src_of, dst):
        local = pltpu.make_async_copy(src_of(me), dst, local_sem.at[stage, s])
        local.start()
        copies = [local]
        for k in range(1, n):
            peer = lax.rem(me + k, n)
            copy = pltpu.make_async_remote_copy(
                src_ref=src_of(peer),
                dst_ref=dst,
                send_sem=send_sem.at[stage, s, k],
                recv_sem=recv_sem.at[stage, s, k],
                device_id={"term": peer},
                device_id_type=MESH,
            )
            copy.start()
            copies.append(copy)
        return copies

    def arrived(copies):
        copies[0].wait()
        for copy in copies[1:]:
            copy.wait_recv()

    def gathered(buf, s, k):
        return buf[s, lax.rem(me + k, n)]

    first = [send(0, s, lambda p, s=s: r_ref.at[s, rows_of(p, share_rows)], got_right.at[s, me]) for s in range(sec_dev)]
    slot_count = sec_dev * channels
    owner_of = [target_ref[i // channels, i % channels] // sec_dev for i in range(slot_count)]
    for i in range(slot_count):
        rank = 0
        for j in range(i):
            rank = rank + jnp.where(owner_of[j] == owner_of[i], 1, 0)
        key_tab[i] = owner_of[i] * capacity + rank
        label_tab[i] = (target_ref[i // channels, i % channels] % sec_dev + 1).astype(jnp.float32)

    def fill_row(q, carry):
        found = jnp.int32(slot_count)
        label = jnp.float32(0.0)
        for i in range(slot_count):
            hit = key_tab[i] == q
            found = jnp.where(hit, i, found)
            label = jnp.where(hit, label_tab[i], label)
        source_tab[q] = found
        slot_label[q] = label
        return carry

    lax.fori_loop(0, owners * capacity, fill_row, 0)
    lanes = lax.broadcasted_iota(jnp.int32, (1, block_size), 1)

    def fill_labels(o, carry):
        row = jnp.zeros((1, block_size), jnp.float32)
        for slot in range(capacity):
            row = jnp.where(lanes == slot, slot_label[o * capacity + slot], row)
        label_rows[o] = row
        return carry

    lax.fori_loop(0, owners, fill_labels, 0)
    labels = route(lambda p: label_rows.at[p], got_labels.at[here], label_sem, load_sem.at[2])
    for load in loads:
        load.wait()
    for s in range(sec_dev):
        l_ref[s] = jnp.dot(l_ref[s], psi_ref[s], precision=PRECISE, preferred_element_type=jnp.float32)

    second = []
    for s in range(sec_dev):
        arrived(first[s])
        parts = [gathered(got_right, s, k) for k in range(n)]
        for a in range(n):
            total = coup_ref[a, me] * parts[0]
            for k in range(1, n):
                total = total + coup_ref[a, lax.rem(me + k, n)] * parts[k]
            comp_rows[s, a] = total
        second.append(send(1, s, lambda p, s=s: comp_rows.at[s, p], comp.at[s, rows_of(me, share_rows)]))
    third = []
    for s in range(sec_dev):
        arrived(second[s])
        contrib[s] = jnp.dot(l_ref[s], comp[s], precision=PRECISE, preferred_element_type=jnp.float32)
        third.append(send(2, s, lambda p, s=s: contrib.at[s, rows_of(p, share_rows)], got_contrib.at[s, me]))
    for s in range(sec_dev):
        terms = [lax.rem(me + k, n) for k in range(n)]
        lives = [
            [jnp.where(channel_ref[terms[k]] == c, pattern_ref[s, terms[k]], 0).astype(jnp.float32) for k in range(n)]
            for c in range(channels)
        ]
        arrived(third[s])
        parts = [gathered(got_contrib, s, k) for k in range(n)]
        for c in range(channels):
            total = lives[c][0] * parts[0]
            for k in range(1, n):
                total = total + lives[c][k] * parts[k]
            partial[s * channels + c] = total
    partial[sec_dev * channels] = jnp.zeros((share_rows, block_size), jnp.float32)
    for o in range(owners):
        for slot in range(capacity):
            at = o * capacity + slot
            outgoing[o, pl.ds(slot * share_rows, share_rows)] = partial[source_tab[at]]
    fourth = route(lambda p: outgoing.at[p], got_slots.at[here], route_sem, load_sem.at[3])
    arrived(labels)
    totals = [None] * sec_dev
    for k in range(owners):
        if k == 0:
            fourth[0].wait()
        else:
            fourth[k].wait_recv()
        o = lax.rem(here + owners - k, owners)
        label_row = got_labels[o]
        for slot in range(capacity):
            label = jnp.broadcast_to(label_row[:, slot:slot + 1], (share_rows, block_size))
            rows = got_slots[o, pl.ds(slot * share_rows, share_rows)]
            for p in range(sec_dev):
                part = jnp.where(label == float(p + 1), rows, 0.0)
                totals[p] = part if totals[p] is None else totals[p] + part
    for p in range(sec_dev):
        out_ref[p] = totals[p]
    for copies in first + second + third + [labels, fourth]:
        for copy in copies[1:]:
            copy.wait_send()


def term_stage(rights, lefts, psi_blocks, couplings, pattern, channel, target, owners):
    sec_dev, block_size, _ = psi_blocks.shape
    n = couplings.shape[0]
    channels = target.shape[1]
    capacity = max(2, (sec_dev * channels + owners - 1) // owners)
    share_rows = block_size // n
    tiles = (sec_dev, n, share_rows, block_size)
    blocks = (sec_dev, block_size, block_size)
    routed = (owners, capacity * share_rows, block_size)
    hbm = pl.BlockSpec(memory_space=pl.ANY)
    smem = pl.BlockSpec(memory_space=pltpu.SMEM)
    vmem = pl.BlockSpec(memory_space=pltpu.VMEM)
    return pl.pallas_call(
        functools.partial(term_kernel, n, owners),
        out_shape=jax.ShapeDtypeStruct((sec_dev, share_rows, block_size), jnp.float32),
        in_specs=[hbm, hbm, hbm, smem, smem, smem, smem],
        out_specs=vmem,
        scratch_shapes=[
            pltpu.VMEM(routed, jnp.float32),
            pltpu.VMEM((owners, 1, block_size), jnp.float32),
            pltpu.VMEM((owners, 1, block_size), jnp.float32),
            pltpu.SMEM((sec_dev * channels,), jnp.int32),
            pltpu.SMEM((sec_dev * channels,), jnp.float32),
            pltpu.SMEM((owners * capacity,), jnp.int32),
            pltpu.SMEM((owners * capacity,), jnp.float32),
            pltpu.VMEM(blocks, jnp.float32),
            pltpu.VMEM(blocks, jnp.float32),
            pltpu.VMEM(tiles, jnp.float32),
            pltpu.VMEM(tiles, jnp.float32),
            pltpu.VMEM(blocks, jnp.float32),
            pltpu.VMEM(blocks, jnp.float32),
            pltpu.VMEM(tiles, jnp.float32),
            pltpu.VMEM((sec_dev * channels + 1, share_rows, block_size), jnp.float32),
            pltpu.VMEM(routed, jnp.float32),
            pltpu.SemaphoreType.DMA((3, sec_dev, n)),
            pltpu.SemaphoreType.DMA((3, sec_dev, n)),
            pltpu.SemaphoreType.DMA((3, sec_dev)),
            pltpu.SemaphoreType.DMA((4,)),
            pltpu.SemaphoreType.DMA((2, owners)),
            pltpu.SemaphoreType.DMA((2, owners)),
        ],
        compiler_params=pltpu.CompilerParams(collective_id=0, has_side_effects=True),
    )(rights, lefts, psi_blocks, couplings, pattern, channel, target)


def local(psi_blocks, left_ops, right_ops, couplings, pattern, channel, target):
    owners = lax.axis_size("sector")
    return term_stage(right_ops[0], left_ops[0], psi_blocks, couplings, pattern.T, channel, target, owners)


def solution(mesh):
    placed = (
        P("sector", None, None),
        P("term", "sector", None, None),
        P("term", "sector", None, None),
        P(),
        P(None, "sector"),
        P(),
        P("sector", None),
    )
    return jax.shard_map(
        local, mesh=mesh, in_specs=placed, out_specs=P("sector", "term", None), check_vma=False
    )
```

```python
import functools

import jax
import jax.numpy as jnp
from jax import lax
from jax.experimental import pallas as pl
from jax.experimental.pallas import tpu as pltpu
from jax.sharding import PartitionSpec as P

MESH = pl.DeviceIdType.MESH

PRECISE = lax.Precision.HIGHEST


def rows_of(index, share_rows):
    return pl.ds(pl.multiple_of(index * share_rows, share_rows), share_rows)


def term_kernel(
    n, owners, r_ref, l_hbm, psi_hbm, coup_ref, pattern_ref, channel_ref, target_ref,
    out_ref,
    got_slots, got_labels, label_rows, key_tab, label_tab, source_tab, slot_label, r_vmem, l_ref, psi_ref, got_right, comp_rows, comp, contrib, got_contrib, partial, outgoing,
    send_sem, recv_sem, local_sem, load_sem, route_sem, label_sem,
):
    me = lax.axis_index("term")
    here = lax.axis_index("sector")
    sec_dev, _, share_rows, block_size = got_right.shape
    channels = (partial.shape[0] - 1) // sec_dev
    capacity = outgoing.shape[1] // share_rows
    right_load = pltpu.make_async_copy(r_ref, r_vmem, load_sem.at[4])
    right_load.start()
    loads = [pltpu.make_async_copy(l_hbm, l_ref, load_sem.at[0]), pltpu.make_async_copy(psi_hbm, psi_ref, load_sem.at[1])]
    for load in loads:
        load.start()
    barrier = pltpu.get_barrier_semaphore()
    for k in range(1, n):
        pl.semaphore_signal(barrier, inc=1, device_id={"term": lax.rem(me + k, n)}, device_id_type=MESH)
    for k in range(1, owners):
        pl.semaphore_signal(barrier, inc=1, device_id={"sector": lax.rem(here + k, owners)}, device_id_type=MESH)
    pl.semaphore_wait(barrier, n - 1 + owners - 1)

    def route(src_of, dst, sems, local):
        first = pltpu.make_async_copy(src_of(here), dst, local)
        first.start()
        copies = [first]
        for k in range(1, owners):
            peer = lax.rem(here + k, owners)
            copy = pltpu.make_async_remote_copy(
                src_ref=src_of(peer),
                dst_ref=dst,
                send_sem=sems.at[0, k],
                recv_sem=sems.at[1, k],
                device_id={"sector": peer},
                device_id_type=MESH,
            )
            copy.start()
            copies.append(copy)
        return copies


    def send(stage, s, src_of, dst):
        local = pltpu.make_async_copy(src_of(me), dst, local_sem.at[stage, s])
        local.start()
        copies = [local]
        for k in range(1, n):
            peer = lax.rem(me + k, n)
            copy = pltpu.make_async_remote_copy(
                src_ref=src_of(peer),
                dst_ref=dst,
                send_sem=send_sem.at[stage, s, k],
                recv_sem=recv_sem.at[stage, s, k],
                device_id={"term": peer},
                device_id_type=MESH,
            )
            copy.start()
            copies.append(copy)
        return copies

    def arrived(copies):
        copies[0].wait()
        for copy in copies[1:]:
            copy.wait_recv()

    def gathered(buf, s, k):
        return buf[s, lax.rem(me + k, n)]

    right_load.wait()
    first = [send(0, s, lambda p, s=s: r_vmem.at[s, rows_of(p, share_rows)], got_right.at[s, me]) for s in range(sec_dev)]
    slot_count = sec_dev * channels
    owner_of = [target_ref[i // channels, i % channels] // sec_dev for i in range(slot_count)]
    for i in range(slot_count):
        rank = 0
        for j in range(i):
            rank = rank + jnp.where(owner_of[j] == owner_of[i], 1, 0)
        key_tab[i] = owner_of[i] * capacity + rank
        label_tab[i] = (target_ref[i // channels, i % channels] % sec_dev + 1).astype(jnp.float32)

    def fill_row(q, carry):
        found = jnp.int32(slot_count)
        label = jnp.float32(0.0)
        for i in range(slot_count):
            hit = key_tab[i] == q
            found = jnp.where(hit, i, found)
            label = jnp.where(hit, label_tab[i], label)
        source_tab[q] = found
        slot_label[q] = label
        return carry

    lax.fori_loop(0, owners * capacity, fill_row, 0)
    lanes = lax.broadcasted_iota(jnp.int32, (1, block_size), 1)

    def fill_labels(o, carry):
        row = jnp.zeros((1, block_size), jnp.float32)
        for slot in range(capacity):
            row = jnp.where(lanes == slot, slot_label[o * capacity + slot], row)
        label_rows[o] = row
        return carry

    lax.fori_loop(0, owners, fill_labels, 0)
    labels = route(lambda p: label_rows.at[p], got_labels.at[here], label_sem, load_sem.at[2])
    for load in loads:
        load.wait()
    for s in range(sec_dev):
        l_ref[s] = jnp.dot(l_ref[s], psi_ref[s], precision=PRECISE, preferred_element_type=jnp.float32)

    second = []
    for s in range(sec_dev):
        arrived(first[s])
        parts = [gathered(got_right, s, k) for k in range(n)]
        for a in range(n):
            total = coup_ref[a, me] * parts[0]
            for k in range(1, n):
                total = total + coup_ref[a, lax.rem(me + k, n)] * parts[k]
            comp_rows[s, a] = total
        second.append(send(1, s, lambda p, s=s: comp_rows.at[s, p], comp.at[s, rows_of(me, share_rows)]))
    third = []
    for s in range(sec_dev):
        arrived(second[s])
        contrib[s] = jnp.dot(l_ref[s], comp[s], precision=PRECISE, preferred_element_type=jnp.float32)
        third.append(send(2, s, lambda p, s=s: contrib.at[s, rows_of(p, share_rows)], got_contrib.at[s, me]))
    for s in range(sec_dev):
        arrived(third[s])
        parts = [gathered(got_contrib, s, k) for k in range(n)]
        for c in range(channels):
            total = None
            for k in range(n):
                term = lax.rem(me + k, n)
                live = jnp.where(channel_ref[term] == c, pattern_ref[s, term], 0).astype(jnp.float32)
                total = live * parts[k] if total is None else total + live * parts[k]
            partial[s * channels + c] = total
    partial[sec_dev * channels] = jnp.zeros((share_rows, block_size), jnp.float32)
    for o in range(owners):
        for slot in range(capacity):
            at = o * capacity + slot
            outgoing[o, pl.ds(slot * share_rows, share_rows)] = partial[source_tab[at]]
    fourth = route(lambda p: outgoing.at[p], got_slots.at[here], route_sem, load_sem.at[3])
    for copies in (labels, fourth):
        arrived(copies)
    totals = [None] * sec_dev
    for o in range(owners):
        label_row = got_labels[o]
        for slot in range(capacity):
            label = jnp.broadcast_to(label_row[:, slot:slot + 1], (share_rows, block_size))
            rows = got_slots[o, pl.ds(slot * share_rows, share_rows)]
            for p in range(sec_dev):
                part = jnp.where(label == float(p + 1), rows, 0.0)
                totals[p] = part if totals[p] is None else totals[p] + part
    for p in range(sec_dev):
        out_ref[p] = totals[p]
    for copies in first + second + third + [labels, fourth]:
        for copy in copies[1:]:
            copy.wait_send()


def term_stage(rights, lefts, psi_blocks, couplings, pattern, channel, target, owners):
    sec_dev, block_size, _ = psi_blocks.shape
    n = couplings.shape[0]
    channels = target.shape[1]
    capacity = max(2, (sec_dev * channels + owners - 1) // owners)
    share_rows = block_size // n
    tiles = (sec_dev, n, share_rows, block_size)
    blocks = (sec_dev, block_size, block_size)
    routed = (owners, capacity * share_rows, block_size)
    hbm = pl.BlockSpec(memory_space=pl.ANY)
    smem = pl.BlockSpec(memory_space=pltpu.SMEM)
    vmem = pl.BlockSpec(memory_space=pltpu.VMEM)
    return pl.pallas_call(
        functools.partial(term_kernel, n, owners),
        out_shape=jax.ShapeDtypeStruct((sec_dev, share_rows, block_size), jnp.float32),
        in_specs=[hbm, hbm, hbm, smem, smem, smem, smem],
        out_specs=vmem,
        scratch_shapes=[
            pltpu.VMEM(routed, jnp.float32),
            pltpu.VMEM((owners, 1, block_size), jnp.float32),
            pltpu.VMEM((owners, 1, block_size), jnp.float32),
            pltpu.SMEM((sec_dev * channels,), jnp.int32),
            pltpu.SMEM((sec_dev * channels,), jnp.float32),
            pltpu.SMEM((owners * capacity,), jnp.int32),
            pltpu.SMEM((owners * capacity,), jnp.float32),
            pltpu.VMEM(blocks, jnp.float32),
            pltpu.VMEM(blocks, jnp.float32),
            pltpu.VMEM(blocks, jnp.float32),
            pltpu.VMEM(tiles, jnp.float32),
            pltpu.VMEM(tiles, jnp.float32),
            pltpu.VMEM(blocks, jnp.float32),
            pltpu.VMEM(blocks, jnp.float32),
            pltpu.VMEM(tiles, jnp.float32),
            pltpu.VMEM((sec_dev * channels + 1, share_rows, block_size), jnp.float32),
            pltpu.VMEM(routed, jnp.float32),
            pltpu.SemaphoreType.DMA((3, sec_dev, n)),
            pltpu.SemaphoreType.DMA((3, sec_dev, n)),
            pltpu.SemaphoreType.DMA((3, sec_dev)),
            pltpu.SemaphoreType.DMA((5,)),
            pltpu.SemaphoreType.DMA((2, owners)),
            pltpu.SemaphoreType.DMA((2, owners)),
        ],
        compiler_params=pltpu.CompilerParams(collective_id=0, has_side_effects=True),
    )(rights, lefts, psi_blocks, couplings, pattern, channel, target)


def local(psi_blocks, left_ops, right_ops, couplings, pattern, channel, target):
    owners = lax.axis_size("sector")
    return term_stage(right_ops[0], left_ops[0], psi_blocks, couplings, pattern.T, channel, target, owners)


def solution(mesh):
    placed = (
        P("sector", None, None),
        P("term", "sector", None, None),
        P("term", "sector", None, None),
        P(),
        P(None, "sector"),
        P(),
        P("sector", None),
    )
    return jax.shard_map(
        local, mesh=mesh, in_specs=placed, out_specs=P("sector", "term", None), check_vma=False
    )
```

```python
import functools

import jax
import jax.numpy as jnp
from jax import lax
from jax.experimental import pallas as pl
from jax.experimental.pallas import tpu as pltpu
from jax.sharding import PartitionSpec as P

MESH = pl.DeviceIdType.MESH

PRECISE = lax.Precision.HIGHEST


def rows_of(index, share_rows):
    return pl.ds(pl.multiple_of(index * share_rows, share_rows), share_rows)


def term_kernel(
    n, owners, r_ref, l_hbm, psi_hbm, coup_ref, pattern_ref, channel_ref, target_ref,
    out_ref,
    got_slots, got_labels, label_rows, key_tab, label_tab, source_tab, slot_label, l_ref, psi_ref, got_right, comp_rows, comp, contrib, got_contrib, partial, outgoing,
    send_sem, recv_sem, local_sem, load_sem, route_sem, label_sem,
):
    me = lax.axis_index("term")
    here = lax.axis_index("sector")
    sec_dev, _, share_rows, block_size = got_right.shape
    channels = (partial.shape[0] - 1) // sec_dev
    capacity = outgoing.shape[1] // share_rows
    loads = [pltpu.make_async_copy(l_hbm, l_ref, load_sem.at[0]), pltpu.make_async_copy(psi_hbm, psi_ref, load_sem.at[1])]
    for load in loads:
        load.start()
    barrier = pltpu.get_barrier_semaphore()
    for k in range(1, n):
        pl.semaphore_signal(barrier, inc=1, device_id={"term": lax.rem(me + k, n)}, device_id_type=MESH)
    for k in range(1, owners):
        pl.semaphore_signal(barrier, inc=1, device_id={"sector": lax.rem(here + k, owners)}, device_id_type=MESH)
    pl.semaphore_wait(barrier, n - 1 + owners - 1)

    def route(src_of, dst, sems, local):
        first = pltpu.make_async_copy(src_of(here), dst, local)
        first.start()
        copies = [first]
        for k in range(1, owners):
            peer = lax.rem(here + k, owners)
            copy = pltpu.make_async_remote_copy(
                src_ref=src_of(peer),
                dst_ref=dst,
                send_sem=sems.at[0, k],
                recv_sem=sems.at[1, k],
                device_id={"sector": peer},
                device_id_type=MESH,
            )
            copy.start()
            copies.append(copy)
        return copies


    def send(stage, s, src_of, dst):
        local = pltpu.make_async_copy(src_of(me), dst, local_sem.at[stage, s])
        local.start()
        copies = [local]
        for k in range(1, n):
            peer = lax.rem(me + k, n)
            copy = pltpu.make_async_remote_copy(
                src_ref=src_of(peer),
                dst_ref=dst,
                send_sem=send_sem.at[stage, s, k],
                recv_sem=recv_sem.at[stage, s, k],
                device_id={"term": peer},
                device_id_type=MESH,
            )
            copy.start()
            copies.append(copy)
        return copies

    def arrived(copies):
        copies[0].wait()
        for copy in copies[1:]:
            copy.wait_recv()

    def gathered(buf, s, k):
        return buf[s, lax.rem(me + k, n)]

    first = [send(0, s, lambda p, s=s: r_ref.at[s, rows_of(p, share_rows)], got_right.at[s, me]) for s in range(sec_dev)]
    for load in loads:
        load.wait()
    for s in range(sec_dev):
        l_ref[s] = jnp.dot(l_ref[s], psi_ref[s], precision=PRECISE, preferred_element_type=jnp.float32)

    second = []
    for s in range(sec_dev):
        arrived(first[s])
        parts = [gathered(got_right, s, k) for k in range(n)]
        for a in range(n):
            total = coup_ref[a, me] * parts[0]
            for k in range(1, n):
                total = total + coup_ref[a, lax.rem(me + k, n)] * parts[k]
            comp_rows[s, a] = total
        second.append(send(1, s, lambda p, s=s: comp_rows.at[s, p], comp.at[s, rows_of(me, share_rows)]))
    third = []
    for s in range(sec_dev):
        arrived(second[s])
        contrib[s] = jnp.dot(l_ref[s], comp[s], precision=PRECISE, preferred_element_type=jnp.float32)
        third.append(send(2, s, lambda p, s=s: contrib.at[s, rows_of(p, share_rows)], got_contrib.at[s, me]))
    slot_count = sec_dev * channels
    owner_of = [target_ref[i // channels, i % channels] // sec_dev for i in range(slot_count)]
    for i in range(slot_count):
        rank = 0
        for j in range(i):
            rank = rank + jnp.where(owner_of[j] == owner_of[i], 1, 0)
        key_tab[i] = owner_of[i] * capacity + rank
        label_tab[i] = (target_ref[i // channels, i % channels] % sec_dev + 1).astype(jnp.float32)

    def fill_row(q, carry):
        found = jnp.int32(slot_count)
        label = jnp.float32(0.0)
        for i in range(slot_count):
            hit = key_tab[i] == q
            found = jnp.where(hit, i, found)
            label = jnp.where(hit, label_tab[i], label)
        source_tab[q] = found
        slot_label[q] = label
        return carry

    lax.fori_loop(0, owners * capacity, fill_row, 0)
    lanes = lax.broadcasted_iota(jnp.int32, (1, block_size), 1)

    def fill_labels(o, carry):
        row = jnp.zeros((1, block_size), jnp.float32)
        for slot in range(capacity):
            row = jnp.where(lanes == slot, slot_label[o * capacity + slot], row)
        label_rows[o] = row
        return carry

    lax.fori_loop(0, owners, fill_labels, 0)
    labels = route(lambda p: label_rows.at[p], got_labels.at[here], label_sem, load_sem.at[2])
    for s in range(sec_dev):
        arrived(third[s])
        parts = [gathered(got_contrib, s, k) for k in range(n)]
        for c in range(channels):
            total = None
            for k in range(n):
                term = lax.rem(me + k, n)
                live = jnp.where(channel_ref[term] == c, pattern_ref[s, term], 0).astype(jnp.float32)
                total = live * parts[k] if total is None else total + live * parts[k]
            partial[s * channels + c] = total
    partial[sec_dev * channels] = jnp.zeros((share_rows, block_size), jnp.float32)
    for o in range(owners):
        for slot in range(capacity):
            at = o * capacity + slot
            outgoing[o, pl.ds(slot * share_rows, share_rows)] = partial[source_tab[at]]
    fourth = route(lambda p: outgoing.at[p], got_slots.at[here], route_sem, load_sem.at[3])
    for copies in (labels, fourth):
        arrived(copies)
    totals = [None] * sec_dev
    for o in range(owners):
        label_row = got_labels[o]
        for slot in range(capacity):
            label = jnp.broadcast_to(label_row[:, slot:slot + 1], (share_rows, block_size))
            rows = got_slots[o, pl.ds(slot * share_rows, share_rows)]
            for p in range(sec_dev):
                part = jnp.where(label == float(p + 1), rows, 0.0)
                totals[p] = part if totals[p] is None else totals[p] + part
    for p in range(sec_dev):
        out_ref[p] = totals[p]
    for copies in first + second + third + [labels, fourth]:
        for copy in copies[1:]:
            copy.wait_send()


def term_stage(rights, lefts, psi_blocks, couplings, pattern, channel, target, owners):
    sec_dev, block_size, _ = psi_blocks.shape
    n = couplings.shape[0]
    channels = target.shape[1]
    capacity = max(2, (sec_dev * channels + owners - 1) // owners)
    share_rows = block_size // n
    tiles = (sec_dev, n, share_rows, block_size)
    blocks = (sec_dev, block_size, block_size)
    routed = (owners, capacity * share_rows, block_size)
    hbm = pl.BlockSpec(memory_space=pl.ANY)
    smem = pl.BlockSpec(memory_space=pltpu.SMEM)
    vmem = pl.BlockSpec(memory_space=pltpu.VMEM)
    return pl.pallas_call(
        functools.partial(term_kernel, n, owners),
        out_shape=jax.ShapeDtypeStruct((sec_dev, share_rows, block_size), jnp.float32),
        in_specs=[hbm, hbm, hbm, smem, smem, smem, smem],
        out_specs=vmem,
        scratch_shapes=[
            pltpu.VMEM(routed, jnp.float32),
            pltpu.VMEM((owners, 1, block_size), jnp.float32),
            pltpu.VMEM((owners, 1, block_size), jnp.float32),
            pltpu.SMEM((sec_dev * channels,), jnp.int32),
            pltpu.SMEM((sec_dev * channels,), jnp.float32),
            pltpu.SMEM((owners * capacity,), jnp.int32),
            pltpu.SMEM((owners * capacity,), jnp.float32),
            pltpu.VMEM(blocks, jnp.float32),
            pltpu.VMEM(blocks, jnp.float32),
            pltpu.VMEM(tiles, jnp.float32),
            pltpu.VMEM(tiles, jnp.float32),
            pltpu.VMEM(blocks, jnp.float32),
            pltpu.VMEM(blocks, jnp.float32),
            pltpu.VMEM(tiles, jnp.float32),
            pltpu.VMEM((sec_dev * channels + 1, share_rows, block_size), jnp.float32),
            pltpu.VMEM(routed, jnp.float32),
            pltpu.SemaphoreType.DMA((3, sec_dev, n)),
            pltpu.SemaphoreType.DMA((3, sec_dev, n)),
            pltpu.SemaphoreType.DMA((3, sec_dev)),
            pltpu.SemaphoreType.DMA((4,)),
            pltpu.SemaphoreType.DMA((2, owners)),
            pltpu.SemaphoreType.DMA((2, owners)),
        ],
        compiler_params=pltpu.CompilerParams(collective_id=0, has_side_effects=True),
    )(rights, lefts, psi_blocks, couplings, pattern, channel, target)


def local(psi_blocks, left_ops, right_ops, couplings, pattern, channel, target):
    owners = lax.axis_size("sector")
    return term_stage(right_ops[0], left_ops[0], psi_blocks, couplings, pattern.T, channel, target, owners)


def solution(mesh):
    placed = (
        P("sector", None, None),
        P("term", "sector", None, None),
        P("term", "sector", None, None),
        P(),
        P(None, "sector"),
        P(),
        P("sector", None),
    )
    return jax.shard_map(
        local, mesh=mesh, in_specs=placed, out_specs=P("sector", "term", None), check_vma=False
    )
```

```python
import functools

import jax
import jax.numpy as jnp
from jax import lax
from jax.experimental import pallas as pl
from jax.experimental.pallas import tpu as pltpu
from jax.sharding import PartitionSpec as P

MESH = pl.DeviceIdType.MESH

PRECISE = lax.Precision.HIGHEST


def rows_of(index, share_rows):
    return pl.ds(pl.multiple_of(index * share_rows, share_rows), share_rows)


def term_kernel(
    n, owners, r_ref, l_hbm, psi_hbm, coup_ref, pattern_ref, channel_ref, target_ref,
    out_ref,
    got_slots, got_labels, label_rows, key_tab, label_tab, source_tab, slot_label, l_ref, psi_ref, got_right, comp_rows, comp, contrib, got_contrib, partial, outgoing,
    send_sem, recv_sem, local_sem, load_sem, route_sem, label_sem,
):
    me = lax.axis_index("term")
    here = lax.axis_index("sector")
    sec_dev, _, share_rows, block_size = got_right.shape
    channels = (partial.shape[0] - 1) // sec_dev
    capacity = outgoing.shape[1] // share_rows
    loads = [pltpu.make_async_copy(l_hbm, l_ref, load_sem.at[0]), pltpu.make_async_copy(psi_hbm, psi_ref, load_sem.at[1])]
    for load in loads:
        load.start()
    barrier = pltpu.get_barrier_semaphore()
    for k in range(1, n):
        pl.semaphore_signal(barrier, inc=1, device_id={"term": lax.rem(me + k, n)}, device_id_type=MESH)
    for k in range(1, owners):
        pl.semaphore_signal(barrier, inc=1, device_id={"sector": lax.rem(here + k, owners)}, device_id_type=MESH)
    pl.semaphore_wait(barrier, n - 1 + owners - 1)

    def route(src_of, dst, sems, local):
        first = pltpu.make_async_copy(src_of(here), dst, local)
        first.start()
        copies = [first]
        for k in range(1, owners):
            peer = lax.rem(here + k, owners)
            copy = pltpu.make_async_remote_copy(
                src_ref=src_of(peer),
                dst_ref=dst,
                send_sem=sems.at[0, k],
                recv_sem=sems.at[1, k],
                device_id={"sector": peer},
                device_id_type=MESH,
            )
            copy.start()
            copies.append(copy)
        return copies


    def send(stage, s, src_of, dst):
        local = pltpu.make_async_copy(src_of(me), dst, local_sem.at[stage, s])
        local.start()
        copies = [local]
        for k in range(1, n):
            peer = lax.rem(me + k, n)
            copy = pltpu.make_async_remote_copy(
                src_ref=src_of(peer),
                dst_ref=dst,
                send_sem=send_sem.at[stage, s, k],
                recv_sem=recv_sem.at[stage, s, k],
                device_id={"term": peer},
                device_id_type=MESH,
            )
            copy.start()
            copies.append(copy)
        return copies

    def arrived(copies):
        copies[0].wait()
        for copy in copies[1:]:
            copy.wait_recv()

    def gathered(buf, s, k):
        return buf[s, lax.rem(me + k, n)]

    first = [send(0, s, lambda p, s=s: r_ref.at[s, rows_of(p, share_rows)], got_right.at[s, me]) for s in range(sec_dev)]
    slot_count = sec_dev * channels
    owner_of = [target_ref[i // channels, i % channels] // sec_dev for i in range(slot_count)]
    for i in range(slot_count):
        rank = 0
        for j in range(i):
            rank = rank + jnp.where(owner_of[j] == owner_of[i], 1, 0)
        key_tab[i] = owner_of[i] * capacity + rank
        label_tab[i] = (target_ref[i // channels, i % channels] % sec_dev + 1).astype(jnp.float32)

    def fill_row(q, carry):
        found = jnp.int32(slot_count)
        label = jnp.float32(0.0)
        for i in range(slot_count):
            hit = key_tab[i] == q
            found = jnp.where(hit, i, found)
            label = jnp.where(hit, label_tab[i], label)
        source_tab[q] = found
        slot_label[q] = label
        return carry

    lax.fori_loop(0, owners * capacity, fill_row, 0)
    lanes = lax.broadcasted_iota(jnp.int32, (1, block_size), 1)

    def fill_labels(o, carry):
        row = jnp.zeros((1, block_size), jnp.float32)
        for slot in range(capacity):
            row = jnp.where(lanes == slot, slot_label[o * capacity + slot], row)
        label_rows[o] = row
        return carry

    lax.fori_loop(0, owners, fill_labels, 0)
    labels = route(lambda p: label_rows.at[p], got_labels.at[here], label_sem, load_sem.at[2])
    for load in loads:
        load.wait()
    for s in range(sec_dev):
        l_ref[s] = jnp.dot(l_ref[s], psi_ref[s], precision=PRECISE, preferred_element_type=jnp.float32)

    second = []
    for s in range(sec_dev):
        arrived(first[s])
        parts = [gathered(got_right, s, k) for k in range(n)]
        for a in range(n):
            total = coup_ref[a, me] * parts[0]
            for k in range(1, n):
                total = total + coup_ref[a, lax.rem(me + k, n)] * parts[k]
            comp_rows[s, a] = total
        second.append(send(1, s, lambda p, s=s: comp_rows.at[s, p], comp.at[s, rows_of(me, share_rows)]))
    third = []
    for s in range(sec_dev):
        arrived(second[s])
        contrib[s] = jnp.dot(l_ref[s], comp[s], precision=PRECISE, preferred_element_type=jnp.float32)
        third.append(send(2, s, lambda p, s=s: contrib.at[s, rows_of(p, share_rows)], got_contrib.at[s, me]))
    for s in range(sec_dev):
        arrived(third[s])
        parts = [gathered(got_contrib, s, k) for k in range(n)]
        for c in range(channels):
            total = None
            for k in range(n):
                term = lax.rem(me + k, n)
                live = jnp.where(channel_ref[term] == c, pattern_ref[s, term], 0).astype(jnp.float32)
                total = live * parts[k] if total is None else total + live * parts[k]
            partial[s * channels + c] = total
    partial[sec_dev * channels] = jnp.zeros((share_rows, block_size), jnp.float32)
    for o in range(owners):
        for slot in range(capacity):
            at = o * capacity + slot
            outgoing[o, pl.ds(slot * share_rows, share_rows)] = partial[source_tab[at]]
    fourth = route(lambda p: outgoing.at[p], got_slots.at[here], route_sem, load_sem.at[3])
    for copies in (labels, fourth):
        arrived(copies)
    totals = [[None] * sec_dev for _ in range(capacity)]
    for o in range(owners):
        label_row = got_labels[o]
        for slot in range(capacity):
            label = jnp.broadcast_to(label_row[:, slot:slot + 1], (share_rows, block_size))
            rows = got_slots[o, pl.ds(slot * share_rows, share_rows)]
            for p in range(sec_dev):
                part = jnp.where(label == float(p + 1), rows, 0.0)
                totals[slot][p] = part if totals[slot][p] is None else totals[slot][p] + part
    for slot in range(capacity):
        for p in range(sec_dev):
            out_ref[slot, p] = totals[slot][p]
    for copies in first + second + third + [labels, fourth]:
        for copy in copies[1:]:
            copy.wait_send()


def term_stage(rights, lefts, psi_blocks, couplings, pattern, channel, target, owners):
    sec_dev, block_size, _ = psi_blocks.shape
    n = couplings.shape[0]
    channels = target.shape[1]
    capacity = max(2, (sec_dev * channels + owners - 1) // owners)
    share_rows = block_size // n
    tiles = (sec_dev, n, share_rows, block_size)
    blocks = (sec_dev, block_size, block_size)
    routed = (owners, capacity * share_rows, block_size)
    hbm = pl.BlockSpec(memory_space=pl.ANY)
    smem = pl.BlockSpec(memory_space=pltpu.SMEM)
    vmem = pl.BlockSpec(memory_space=pltpu.VMEM)
    return pl.pallas_call(
        functools.partial(term_kernel, n, owners),
        out_shape=jax.ShapeDtypeStruct((capacity, sec_dev, share_rows, block_size), jnp.float32),
        in_specs=[hbm, hbm, hbm, smem, smem, smem, smem],
        out_specs=vmem,
        scratch_shapes=[
            pltpu.VMEM(routed, jnp.float32),
            pltpu.VMEM((owners, 1, block_size), jnp.float32),
            pltpu.VMEM((owners, 1, block_size), jnp.float32),
            pltpu.SMEM((sec_dev * channels,), jnp.int32),
            pltpu.SMEM((sec_dev * channels,), jnp.float32),
            pltpu.SMEM((owners * capacity,), jnp.int32),
            pltpu.SMEM((owners * capacity,), jnp.float32),
            pltpu.VMEM(blocks, jnp.float32),
            pltpu.VMEM(blocks, jnp.float32),
            pltpu.VMEM(tiles, jnp.float32),
            pltpu.VMEM(tiles, jnp.float32),
            pltpu.VMEM(blocks, jnp.float32),
            pltpu.VMEM(blocks, jnp.float32),
            pltpu.VMEM(tiles, jnp.float32),
            pltpu.VMEM((sec_dev * channels + 1, share_rows, block_size), jnp.float32),
            pltpu.VMEM(routed, jnp.float32),
            pltpu.SemaphoreType.DMA((3, sec_dev, n)),
            pltpu.SemaphoreType.DMA((3, sec_dev, n)),
            pltpu.SemaphoreType.DMA((3, sec_dev)),
            pltpu.SemaphoreType.DMA((4,)),
            pltpu.SemaphoreType.DMA((2, owners)),
            pltpu.SemaphoreType.DMA((2, owners)),
        ],
        compiler_params=pltpu.CompilerParams(collective_id=0, has_side_effects=True),
    )(rights, lefts, psi_blocks, couplings, pattern, channel, target)


def local(psi_blocks, left_ops, right_ops, couplings, pattern, channel, target):
    owners = lax.axis_size("sector")
    by_rank = term_stage(right_ops[0], left_ops[0], psi_blocks, couplings, pattern.T, channel, target, owners)
    return jnp.sum(by_rank, axis=0)


def solution(mesh):
    placed = (
        P("sector", None, None),
        P("term", "sector", None, None),
        P("term", "sector", None, None),
        P(),
        P(None, "sector"),
        P(),
        P("sector", None),
    )
    return jax.shard_map(
        local, mesh=mesh, in_specs=placed, out_specs=P("sector", "term", None), check_vma=False
    )
```

```python
import functools

import jax
import jax.numpy as jnp
from jax import lax
from jax.experimental import pallas as pl
from jax.experimental.pallas import tpu as pltpu
from jax.sharding import PartitionSpec as P

MESH = pl.DeviceIdType.MESH

PRECISE = lax.Precision.HIGHEST


def rows_of(index, share_rows):
    return pl.ds(pl.multiple_of(index * share_rows, share_rows), share_rows)


def term_kernel(
    n, owners, r_ref, l_hbm, psi_hbm, coup_ref, pattern_ref, channel_ref, target_ref,
    out_ref,
    got_slots, got_labels, label_rows, key_tab, label_tab, source_tab, slot_label, l_ref, psi_ref, got_right, comp_rows, comp, contrib, got_contrib, partial, outgoing,
    send_sem, recv_sem, local_sem, load_sem, route_sem, label_sem,
):
    me = lax.axis_index("term")
    here = lax.axis_index("sector")
    sec_dev, _, share_rows, block_size = got_right.shape
    channels = (partial.shape[0] - 1) // sec_dev
    capacity = outgoing.shape[1] // share_rows
    loads = [pltpu.make_async_copy(l_hbm, l_ref, load_sem.at[0]), pltpu.make_async_copy(psi_hbm, psi_ref, load_sem.at[1])]
    for load in loads:
        load.start()
    barrier = pltpu.get_barrier_semaphore()
    for k in range(1, n):
        pl.semaphore_signal(barrier, inc=1, device_id={"term": lax.rem(me + k, n)}, device_id_type=MESH)
    for k in range(1, owners):
        pl.semaphore_signal(barrier, inc=1, device_id={"sector": lax.rem(here + k, owners)}, device_id_type=MESH)
    pl.semaphore_wait(barrier, n - 1 + owners - 1)

    def route(src_of, dst, sems, local):
        first = pltpu.make_async_copy(src_of(here), dst, local)
        first.start()
        copies = [first]
        for k in range(1, owners):
            peer = lax.rem(here + k, owners)
            copy = pltpu.make_async_remote_copy(
                src_ref=src_of(peer),
                dst_ref=dst,
                send_sem=sems.at[0, k],
                recv_sem=sems.at[1, k],
                device_id={"sector": peer},
                device_id_type=MESH,
            )
            copy.start()
            copies.append(copy)
        return copies


    def send(stage, s, src_of, dst):
        local = pltpu.make_async_copy(src_of(me), dst, local_sem.at[stage, s])
        local.start()
        copies = [local]
        for k in range(1, n):
            peer = lax.rem(me + k, n)
            copy = pltpu.make_async_remote_copy(
                src_ref=src_of(peer),
                dst_ref=dst,
                send_sem=send_sem.at[stage, s, k],
                recv_sem=recv_sem.at[stage, s, k],
                device_id={"term": peer},
                device_id_type=MESH,
            )
            copy.start()
            copies.append(copy)
        return copies

    def arrived(copies):
        copies[0].wait()
        for copy in copies[1:]:
            copy.wait_recv()

    def gathered(buf, s, k):
        return buf[s, lax.rem(me + k, n)]

    first = [send(0, s, lambda p, s=s: r_ref.at[s, rows_of(p, share_rows)], got_right.at[s, me]) for s in range(sec_dev)]
    slot_count = sec_dev * channels
    owner_of = [target_ref[i // channels, i % channels] // sec_dev for i in range(slot_count)]
    for i in range(slot_count):
        rank = 0
        for j in range(i):
            rank = rank + jnp.where(owner_of[j] == owner_of[i], 1, 0)
        key_tab[i] = owner_of[i] * capacity + rank
        label_tab[i] = (target_ref[i // channels, i % channels] % sec_dev + 1).astype(jnp.float32)

    def fill_row(q, carry):
        found = jnp.int32(slot_count)
        label = jnp.float32(0.0)
        for i in range(slot_count):
            hit = key_tab[i] == q
            found = jnp.where(hit, i, found)
            label = jnp.where(hit, label_tab[i], label)
        source_tab[q] = found
        slot_label[q] = label
        return carry

    lax.fori_loop(0, owners * capacity, fill_row, 0)
    lanes = lax.broadcasted_iota(jnp.int32, (1, block_size), 1)

    def fill_labels(o, carry):
        row = jnp.zeros((1, block_size), jnp.float32)
        for slot in range(capacity):
            row = jnp.where(lanes == slot, slot_label[o * capacity + slot], row)
        label_rows[o] = row
        return carry

    lax.fori_loop(0, owners, fill_labels, 0)
    labels = route(lambda p: label_rows.at[p], got_labels.at[here], label_sem, load_sem.at[2])
    for load in loads:
        load.wait()
    for s in range(sec_dev):
        l_ref[s] = jnp.dot(l_ref[s], psi_ref[s], precision=PRECISE, preferred_element_type=jnp.float32)

    second = []
    for s in range(sec_dev):
        arrived(first[s])
        parts = [gathered(got_right, s, k) for k in range(n)]
        for a in range(n):
            total = coup_ref[a, me] * parts[0]
            for k in range(1, n):
                total = total + coup_ref[a, lax.rem(me + k, n)] * parts[k]
            comp_rows[s, a] = total
        second.append(send(1, s, lambda p, s=s: comp_rows.at[s, p], comp.at[s, rows_of(me, share_rows)]))
    third = []
    for s in range(sec_dev):
        arrived(second[s])
        contrib[s] = jnp.dot(l_ref[s], comp[s], precision=PRECISE, preferred_element_type=jnp.float32)
        third.append(send(2, s, lambda p, s=s: contrib.at[s, rows_of(p, share_rows)], got_contrib.at[s, me]))
    for s in range(sec_dev):
        arrived(third[s])
        parts = [gathered(got_contrib, s, k) for k in range(n)]
        for c in range(channels):
            total = None
            for k in range(n):
                term = lax.rem(me + k, n)
                live = jnp.where(channel_ref[term] == c, pattern_ref[s, term], 0).astype(jnp.float32)
                total = live * parts[k] if total is None else total + live * parts[k]
            partial[s * channels + c] = total
    partial[sec_dev * channels] = jnp.zeros((share_rows, block_size), jnp.float32)
    fourth = []
    for k in range(owners):
        o = lax.rem(here + k, owners)
        for slot in range(capacity):
            outgoing[o, pl.ds(slot * share_rows, share_rows)] = partial[source_tab[o * capacity + slot]]
        if k == 0:
            copy = pltpu.make_async_copy(outgoing.at[o], got_slots.at[here], load_sem.at[3])
        else:
            copy = pltpu.make_async_remote_copy(
                src_ref=outgoing.at[o],
                dst_ref=got_slots.at[here],
                send_sem=route_sem.at[0, k],
                recv_sem=route_sem.at[1, k],
                device_id={"sector": o},
                device_id_type=MESH,
            )
        copy.start()
        fourth.append(copy)
    for copies in (labels, fourth):
        arrived(copies)
    totals = [None] * sec_dev
    for o in range(owners):
        label_row = got_labels[o]
        for slot in range(capacity):
            label = jnp.broadcast_to(label_row[:, slot:slot + 1], (share_rows, block_size))
            rows = got_slots[o, pl.ds(slot * share_rows, share_rows)]
            for p in range(sec_dev):
                part = jnp.where(label == float(p + 1), rows, 0.0)
                totals[p] = part if totals[p] is None else totals[p] + part
    for p in range(sec_dev):
        out_ref[p] = totals[p]
    for copies in first + second + third + [labels, fourth]:
        for copy in copies[1:]:
            copy.wait_send()


def term_stage(rights, lefts, psi_blocks, couplings, pattern, channel, target, owners):
    sec_dev, block_size, _ = psi_blocks.shape
    n = couplings.shape[0]
    channels = target.shape[1]
    capacity = max(2, (sec_dev * channels + owners - 1) // owners)
    share_rows = block_size // n
    tiles = (sec_dev, n, share_rows, block_size)
    blocks = (sec_dev, block_size, block_size)
    routed = (owners, capacity * share_rows, block_size)
    hbm = pl.BlockSpec(memory_space=pl.ANY)
    smem = pl.BlockSpec(memory_space=pltpu.SMEM)
    vmem = pl.BlockSpec(memory_space=pltpu.VMEM)
    return pl.pallas_call(
        functools.partial(term_kernel, n, owners),
        out_shape=jax.ShapeDtypeStruct((sec_dev, share_rows, block_size), jnp.float32),
        in_specs=[hbm, hbm, hbm, smem, smem, smem, smem],
        out_specs=vmem,
        scratch_shapes=[
            pltpu.VMEM(routed, jnp.float32),
            pltpu.VMEM((owners, 1, block_size), jnp.float32),
            pltpu.VMEM((owners, 1, block_size), jnp.float32),
            pltpu.SMEM((sec_dev * channels,), jnp.int32),
            pltpu.SMEM((sec_dev * channels,), jnp.float32),
            pltpu.SMEM((owners * capacity,), jnp.int32),
            pltpu.SMEM((owners * capacity,), jnp.float32),
            pltpu.VMEM(blocks, jnp.float32),
            pltpu.VMEM(blocks, jnp.float32),
            pltpu.VMEM(tiles, jnp.float32),
            pltpu.VMEM(tiles, jnp.float32),
            pltpu.VMEM(blocks, jnp.float32),
            pltpu.VMEM(blocks, jnp.float32),
            pltpu.VMEM(tiles, jnp.float32),
            pltpu.VMEM((sec_dev * channels + 1, share_rows, block_size), jnp.float32),
            pltpu.VMEM(routed, jnp.float32),
            pltpu.SemaphoreType.DMA((3, sec_dev, n)),
            pltpu.SemaphoreType.DMA((3, sec_dev, n)),
            pltpu.SemaphoreType.DMA((3, sec_dev)),
            pltpu.SemaphoreType.DMA((4,)),
            pltpu.SemaphoreType.DMA((2, owners)),
            pltpu.SemaphoreType.DMA((2, owners)),
        ],
        compiler_params=pltpu.CompilerParams(collective_id=0, has_side_effects=True),
    )(rights, lefts, psi_blocks, couplings, pattern, channel, target)


def local(psi_blocks, left_ops, right_ops, couplings, pattern, channel, target):
    owners = lax.axis_size("sector")
    return term_stage(right_ops[0], left_ops[0], psi_blocks, couplings, pattern.T, channel, target, owners)


def solution(mesh):
    placed = (
        P("sector", None, None),
        P("term", "sector", None, None),
        P("term", "sector", None, None),
        P(),
        P(None, "sector"),
        P(),
        P("sector", None),
    )
    return jax.shard_map(
        local, mesh=mesh, in_specs=placed, out_specs=P("sector", "term", None), check_vma=False
    )
```

```python
import functools

import jax
import jax.numpy as jnp
from jax import lax
from jax.experimental import pallas as pl
from jax.experimental.pallas import tpu as pltpu
from jax.sharding import PartitionSpec as P

MESH = pl.DeviceIdType.MESH

PRECISE = lax.Precision.HIGH


def rows_of(index, share_rows):
    return pl.ds(pl.multiple_of(index * share_rows, share_rows), share_rows)


def term_kernel(
    n, owners, r_ref, l_hbm, psi_hbm, coup_ref, pattern_ref, channel_ref, target_ref,
    out_ref,
    got_slots, got_labels, label_rows, key_tab, label_tab, source_tab, slot_label, l_ref, psi_ref, got_right, comp_rows, comp, contrib, got_contrib, partial, outgoing,
    send_sem, recv_sem, local_sem, load_sem, route_sem, label_sem,
):
    me = lax.axis_index("term")
    here = lax.axis_index("sector")
    sec_dev, _, share_rows, block_size = got_right.shape
    channels = (partial.shape[0] - 1) // sec_dev
    capacity = outgoing.shape[1] // share_rows
    loads = [pltpu.make_async_copy(l_hbm, l_ref, load_sem.at[0]), pltpu.make_async_copy(psi_hbm, psi_ref, load_sem.at[1])]
    for load in loads:
        load.start()
    barrier = pltpu.get_barrier_semaphore()
    for k in range(1, n):
        pl.semaphore_signal(barrier, inc=1, device_id={"term": lax.rem(me + k, n)}, device_id_type=MESH)
    for k in range(1, owners):
        pl.semaphore_signal(barrier, inc=1, device_id={"sector": lax.rem(here + k, owners)}, device_id_type=MESH)
    pl.semaphore_wait(barrier, n - 1 + owners - 1)

    def route(src_of, dst, sems, local):
        first = pltpu.make_async_copy(src_of(here), dst, local)
        first.start()
        copies = [first]
        for k in range(1, owners):
            peer = lax.rem(here + k, owners)
            copy = pltpu.make_async_remote_copy(
                src_ref=src_of(peer),
                dst_ref=dst,
                send_sem=sems.at[0, k],
                recv_sem=sems.at[1, k],
                device_id={"sector": peer},
                device_id_type=MESH,
            )
            copy.start()
            copies.append(copy)
        return copies


    def send(stage, s, src_of, dst):
        local = pltpu.make_async_copy(src_of(me), dst, local_sem.at[stage, s])
        local.start()
        copies = [local]
        for k in range(1, n):
            peer = lax.rem(me + k, n)
            copy = pltpu.make_async_remote_copy(
                src_ref=src_of(peer),
                dst_ref=dst,
                send_sem=send_sem.at[stage, s, k],
                recv_sem=recv_sem.at[stage, s, k],
                device_id={"term": peer},
                device_id_type=MESH,
            )
            copy.start()
            copies.append(copy)
        return copies

    def arrived(copies):
        copies[0].wait()
        for copy in copies[1:]:
            copy.wait_recv()

    def gathered(buf, s, k):
        return buf[s, lax.rem(me + k, n)]

    first = [send(0, s, lambda p, s=s: r_ref.at[s, rows_of(p, share_rows)], got_right.at[s, me]) for s in range(sec_dev)]
    slot_count = sec_dev * channels
    owner_of = [target_ref[i // channels, i % channels] // sec_dev for i in range(slot_count)]
    for i in range(slot_count):
        rank = 0
        for j in range(i):
            rank = rank + jnp.where(owner_of[j] == owner_of[i], 1, 0)
        key_tab[i] = owner_of[i] * capacity + rank
        label_tab[i] = (target_ref[i // channels, i % channels] % sec_dev + 1).astype(jnp.float32)

    def fill_row(q, carry):
        found = jnp.int32(slot_count)
        label = jnp.float32(0.0)
        for i in range(slot_count):
            hit = key_tab[i] == q
            found = jnp.where(hit, i, found)
            label = jnp.where(hit, label_tab[i], label)
        source_tab[q] = found
        slot_label[q] = label
        return carry

    lax.fori_loop(0, owners * capacity, fill_row, 0)
    lanes = lax.broadcasted_iota(jnp.int32, (1, block_size), 1)

    def fill_labels(o, carry):
        row = jnp.zeros((1, block_size), jnp.float32)
        for slot in range(capacity):
            row = jnp.where(lanes == slot, slot_label[o * capacity + slot], row)
        label_rows[o] = row
        return carry

    lax.fori_loop(0, owners, fill_labels, 0)
    labels = route(lambda p: label_rows.at[p], got_labels.at[here], label_sem, load_sem.at[2])
    for load in loads:
        load.wait()
    for s in range(sec_dev):
        l_ref[s] = jnp.dot(l_ref[s], psi_ref[s], precision=PRECISE, preferred_element_type=jnp.float32)

    second = []
    for s in range(sec_dev):
        arrived(first[s])
        parts = [gathered(got_right, s, k) for k in range(n)]
        for a in range(n):
            total = coup_ref[a, me] * parts[0]
            for k in range(1, n):
                total = total + coup_ref[a, lax.rem(me + k, n)] * parts[k]
            comp_rows[s, a] = total
        second.append(send(1, s, lambda p, s=s: comp_rows.at[s, p], comp.at[s, rows_of(me, share_rows)]))
    third = []
    for s in range(sec_dev):
        arrived(second[s])
        contrib[s] = jnp.dot(l_ref[s], comp[s], precision=PRECISE, preferred_element_type=jnp.float32)
        third.append(send(2, s, lambda p, s=s: contrib.at[s, rows_of(p, share_rows)], got_contrib.at[s, me]))
    for s in range(sec_dev):
        arrived(third[s])
        parts = [gathered(got_contrib, s, k) for k in range(n)]
        for c in range(channels):
            total = None
            for k in range(n):
                term = lax.rem(me + k, n)
                live = jnp.where(channel_ref[term] == c, pattern_ref[s, term], 0).astype(jnp.float32)
                total = live * parts[k] if total is None else total + live * parts[k]
            partial[s * channels + c] = total
    partial[sec_dev * channels] = jnp.zeros((share_rows, block_size), jnp.float32)
    for o in range(owners):
        for slot in range(capacity):
            at = o * capacity + slot
            outgoing[o, pl.ds(slot * share_rows, share_rows)] = partial[source_tab[at]]
    fourth = route(lambda p: outgoing.at[p], got_slots.at[here], route_sem, load_sem.at[3])
    for copies in (labels, fourth):
        arrived(copies)
    totals = [None] * sec_dev
    for o in range(owners):
        label_row = got_labels[o]
        for slot in range(capacity):
            label = jnp.broadcast_to(label_row[:, slot:slot + 1], (share_rows, block_size))
            rows = got_slots[o, pl.ds(slot * share_rows, share_rows)]
            for p in range(sec_dev):
                part = jnp.where(label == float(p + 1), rows, 0.0)
                totals[p] = part if totals[p] is None else totals[p] + part
    for p in range(sec_dev):
        out_ref[p] = totals[p]
    for copies in first + second + third + [labels, fourth]:
        for copy in copies[1:]:
            copy.wait_send()


def term_stage(rights, lefts, psi_blocks, couplings, pattern, channel, target, owners):
    sec_dev, block_size, _ = psi_blocks.shape
    n = couplings.shape[0]
    channels = target.shape[1]
    capacity = max(2, (sec_dev * channels + owners - 1) // owners)
    share_rows = block_size // n
    tiles = (sec_dev, n, share_rows, block_size)
    blocks = (sec_dev, block_size, block_size)
    routed = (owners, capacity * share_rows, block_size)
    hbm = pl.BlockSpec(memory_space=pl.ANY)
    smem = pl.BlockSpec(memory_space=pltpu.SMEM)
    vmem = pl.BlockSpec(memory_space=pltpu.VMEM)
    return pl.pallas_call(
        functools.partial(term_kernel, n, owners),
        out_shape=jax.ShapeDtypeStruct((sec_dev, share_rows, block_size), jnp.float32),
        in_specs=[hbm, hbm, hbm, smem, smem, smem, smem],
        out_specs=vmem,
        scratch_shapes=[
            pltpu.VMEM(routed, jnp.float32),
            pltpu.VMEM((owners, 1, block_size), jnp.float32),
            pltpu.VMEM((owners, 1, block_size), jnp.float32),
            pltpu.SMEM((sec_dev * channels,), jnp.int32),
            pltpu.SMEM((sec_dev * channels,), jnp.float32),
            pltpu.SMEM((owners * capacity,), jnp.int32),
            pltpu.SMEM((owners * capacity,), jnp.float32),
            pltpu.VMEM(blocks, jnp.float32),
            pltpu.VMEM(blocks, jnp.float32),
            pltpu.VMEM(tiles, jnp.float32),
            pltpu.VMEM(tiles, jnp.float32),
            pltpu.VMEM(blocks, jnp.float32),
            pltpu.VMEM(blocks, jnp.float32),
            pltpu.VMEM(tiles, jnp.float32),
            pltpu.VMEM((sec_dev * channels + 1, share_rows, block_size), jnp.float32),
            pltpu.VMEM(routed, jnp.float32),
            pltpu.SemaphoreType.DMA((3, sec_dev, n)),
            pltpu.SemaphoreType.DMA((3, sec_dev, n)),
            pltpu.SemaphoreType.DMA((3, sec_dev)),
            pltpu.SemaphoreType.DMA((4,)),
            pltpu.SemaphoreType.DMA((2, owners)),
            pltpu.SemaphoreType.DMA((2, owners)),
        ],
        compiler_params=pltpu.CompilerParams(collective_id=0, has_side_effects=True),
    )(rights, lefts, psi_blocks, couplings, pattern, channel, target)


def local(psi_blocks, left_ops, right_ops, couplings, pattern, channel, target):
    owners = lax.axis_size("sector")
    return term_stage(right_ops[0], left_ops[0], psi_blocks, couplings, pattern.T, channel, target, owners)


def solution(mesh):
    placed = (
        P("sector", None, None),
        P("term", "sector", None, None),
        P("term", "sector", None, None),
        P(),
        P(None, "sector"),
        P(),
        P("sector", None),
    )
    return jax.shard_map(
        local, mesh=mesh, in_specs=placed, out_specs=P("sector", "term", None), check_vma=False
    )
```

```python
import functools

import jax
import jax.numpy as jnp
from jax import lax
from jax.experimental import pallas as pl
from jax.experimental.pallas import tpu as pltpu
from jax.sharding import PartitionSpec as P

MESH = pl.DeviceIdType.MESH

PRECISE = lax.Precision.HIGHEST


def rows_of(index, share_rows):
    return pl.ds(pl.multiple_of(index * share_rows, share_rows), share_rows)


def term_kernel(
    n, owners, r_ref, l_hbm, psi_hbm, coup_ref, pattern_ref, channel_ref, target_ref,
    out_ref,
    got_slots, got_labels, label_rows, key_tab, label_tab, source_tab, slot_label, l_ref, psi_ref, got_right, comp_rows, comp, contrib, got_contrib, partial, outgoing,
    send_sem, recv_sem, local_sem, load_sem, route_sem, label_sem,
):
    me = lax.axis_index("term")
    here = lax.axis_index("sector")
    sec_dev, _, share_rows, block_size = got_right.shape
    channels = (partial.shape[0] - 1) // sec_dev
    capacity = outgoing.shape[1] // share_rows
    loads = [pltpu.make_async_copy(l_hbm, l_ref, load_sem.at[0]), pltpu.make_async_copy(psi_hbm, psi_ref, load_sem.at[1])]
    for load in loads:
        load.start()
    barrier = pltpu.get_barrier_semaphore()
    for k in range(1, n):
        pl.semaphore_signal(barrier, inc=1, device_id={"term": lax.rem(me + k, n)}, device_id_type=MESH)
    for k in range(1, owners):
        pl.semaphore_signal(barrier, inc=1, device_id={"sector": lax.rem(here + k, owners)}, device_id_type=MESH)
    pl.semaphore_wait(barrier, n - 1 + owners - 1)

    def route(src_of, dst, sems, local):
        first = pltpu.make_async_copy(src_of(here), dst, local)
        first.start()
        copies = [first]
        for k in range(1, owners):
            peer = lax.rem(here + k, owners)
            copy = pltpu.make_async_remote_copy(
                src_ref=src_of(peer),
                dst_ref=dst,
                send_sem=sems.at[0, k],
                recv_sem=sems.at[1, k],
                device_id={"sector": peer},
                device_id_type=MESH,
            )
            copy.start()
            copies.append(copy)
        return copies


    def send(stage, s, src_of, dst):
        local = pltpu.make_async_copy(src_of(me), dst, local_sem.at[stage, s])
        local.start()
        copies = [local]
        for k in range(1, n):
            peer = lax.rem(me + k, n)
            copy = pltpu.make_async_remote_copy(
                src_ref=src_of(peer),
                dst_ref=dst,
                send_sem=send_sem.at[stage, s, k],
                recv_sem=recv_sem.at[stage, s, k],
                device_id={"term": peer},
                device_id_type=MESH,
            )
            copy.start()
            copies.append(copy)
        return copies

    def arrived(copies):
        copies[0].wait()
        for copy in copies[1:]:
            copy.wait_recv()

    def gathered(buf, s, k):
        return buf[s, lax.rem(me + k, n)]

    first = [send(0, s, lambda p, s=s: r_ref.at[s, rows_of(p, share_rows)], got_right.at[s, me]) for s in range(sec_dev)]
    slot_count = sec_dev * channels
    owner_of = [target_ref[i // channels, i % channels] // sec_dev for i in range(slot_count)]
    for i in range(slot_count):
        rank = 0
        for j in range(i):
            rank = rank + jnp.where(owner_of[j] == owner_of[i], 1, 0)
        key_tab[i] = owner_of[i] * capacity + rank
        label_tab[i] = (target_ref[i // channels, i % channels] % sec_dev + 1).astype(jnp.float32)

    def fill_row(q, carry):
        found = jnp.int32(slot_count)
        label = jnp.float32(0.0)
        for i in range(slot_count):
            hit = key_tab[i] == q
            found = jnp.where(hit, i, found)
            label = jnp.where(hit, label_tab[i], label)
        source_tab[q] = found
        slot_label[q] = label
        return carry

    lax.fori_loop(0, owners * capacity, fill_row, 0)
    lanes = lax.broadcasted_iota(jnp.int32, (1, block_size), 1)

    def fill_labels(o, carry):
        row = jnp.zeros((1, block_size), jnp.float32)
        for slot in range(capacity):
            row = jnp.where(lanes == slot, slot_label[o * capacity + slot], row)
        label_rows[o] = row
        return carry

    lax.fori_loop(0, owners, fill_labels, 0)
    for load in loads:
        load.wait()
    for s in range(sec_dev):
        l_ref[s] = jnp.dot(l_ref[s], psi_ref[s], precision=PRECISE, preferred_element_type=jnp.float32)

    second = []
    for s in range(sec_dev):
        arrived(first[s])
        parts = [gathered(got_right, s, k) for k in range(n)]
        for a in range(n):
            total = coup_ref[a, me] * parts[0]
            for k in range(1, n):
                total = total + coup_ref[a, lax.rem(me + k, n)] * parts[k]
            comp_rows[s, a] = total
        second.append(send(1, s, lambda p, s=s: comp_rows.at[s, p], comp.at[s, rows_of(me, share_rows)]))
    third = []
    for s in range(sec_dev):
        arrived(second[s])
        contrib[s] = jnp.dot(l_ref[s], comp[s], precision=PRECISE, preferred_element_type=jnp.float32)
        third.append(send(2, s, lambda p, s=s: contrib.at[s, rows_of(p, share_rows)], got_contrib.at[s, me]))
    labels = route(lambda p: label_rows.at[p], got_labels.at[here], label_sem, load_sem.at[2])
    for s in range(sec_dev):
        arrived(third[s])
        parts = [gathered(got_contrib, s, k) for k in range(n)]
        for c in range(channels):
            total = None
            for k in range(n):
                term = lax.rem(me + k, n)
                live = jnp.where(channel_ref[term] == c, pattern_ref[s, term], 0).astype(jnp.float32)
                total = live * parts[k] if total is None else total + live * parts[k]
            partial[s * channels + c] = total
    partial[sec_dev * channels] = jnp.zeros((share_rows, block_size), jnp.float32)
    for o in range(owners):
        for slot in range(capacity):
            at = o * capacity + slot
            outgoing[o, pl.ds(slot * share_rows, share_rows)] = partial[source_tab[at]]
    fourth = route(lambda p: outgoing.at[p], got_slots.at[here], route_sem, load_sem.at[3])
    for copies in (labels, fourth):
        arrived(copies)
    totals = [None] * sec_dev
    for o in range(owners):
        label_row = got_labels[o]
        for slot in range(capacity):
            label = jnp.broadcast_to(label_row[:, slot:slot + 1], (share_rows, block_size))
            rows = got_slots[o, pl.ds(slot * share_rows, share_rows)]
            for p in range(sec_dev):
                part = jnp.where(label == float(p + 1), rows, 0.0)
                totals[p] = part if totals[p] is None else totals[p] + part
    for p in range(sec_dev):
        out_ref[p] = totals[p]
    for copies in first + second + third + [labels, fourth]:
        for copy in copies[1:]:
            copy.wait_send()


def term_stage(rights, lefts, psi_blocks, couplings, pattern, channel, target, owners):
    sec_dev, block_size, _ = psi_blocks.shape
    n = couplings.shape[0]
    channels = target.shape[1]
    capacity = max(2, (sec_dev * channels + owners - 1) // owners)
    share_rows = block_size // n
    tiles = (sec_dev, n, share_rows, block_size)
    blocks = (sec_dev, block_size, block_size)
    routed = (owners, capacity * share_rows, block_size)
    hbm = pl.BlockSpec(memory_space=pl.ANY)
    smem = pl.BlockSpec(memory_space=pltpu.SMEM)
    vmem = pl.BlockSpec(memory_space=pltpu.VMEM)
    return pl.pallas_call(
        functools.partial(term_kernel, n, owners),
        out_shape=jax.ShapeDtypeStruct((sec_dev, share_rows, block_size), jnp.float32),
        in_specs=[hbm, hbm, hbm, smem, smem, smem, smem],
        out_specs=vmem,
        scratch_shapes=[
            pltpu.VMEM(routed, jnp.float32),
            pltpu.VMEM((owners, 1, block_size), jnp.float32),
            pltpu.VMEM((owners, 1, block_size), jnp.float32),
            pltpu.SMEM((sec_dev * channels,), jnp.int32),
            pltpu.SMEM((sec_dev * channels,), jnp.float32),
            pltpu.SMEM((owners * capacity,), jnp.int32),
            pltpu.SMEM((owners * capacity,), jnp.float32),
            pltpu.VMEM(blocks, jnp.float32),
            pltpu.VMEM(blocks, jnp.float32),
            pltpu.VMEM(tiles, jnp.float32),
            pltpu.VMEM(tiles, jnp.float32),
            pltpu.VMEM(blocks, jnp.float32),
            pltpu.VMEM(blocks, jnp.float32),
            pltpu.VMEM(tiles, jnp.float32),
            pltpu.VMEM((sec_dev * channels + 1, share_rows, block_size), jnp.float32),
            pltpu.VMEM(routed, jnp.float32),
            pltpu.SemaphoreType.DMA((3, sec_dev, n)),
            pltpu.SemaphoreType.DMA((3, sec_dev, n)),
            pltpu.SemaphoreType.DMA((3, sec_dev)),
            pltpu.SemaphoreType.DMA((4,)),
            pltpu.SemaphoreType.DMA((2, owners)),
            pltpu.SemaphoreType.DMA((2, owners)),
        ],
        compiler_params=pltpu.CompilerParams(collective_id=0, has_side_effects=True),
    )(rights, lefts, psi_blocks, couplings, pattern, channel, target)


def local(psi_blocks, left_ops, right_ops, couplings, pattern, channel, target):
    owners = lax.axis_size("sector")
    return term_stage(right_ops[0], left_ops[0], psi_blocks, couplings, pattern.T, channel, target, owners)


def solution(mesh):
    placed = (
        P("sector", None, None),
        P("term", "sector", None, None),
        P("term", "sector", None, None),
        P(),
        P(None, "sector"),
        P(),
        P("sector", None),
    )
    return jax.shard_map(
        local, mesh=mesh, in_specs=placed, out_specs=P("sector", "term", None), check_vma=False
    )
```
